256 devices in a mesh: grp: 8 (over x, core), tile: 32 (over z, y).
Axes of the slice: x: 4, y: 4, z: 8, core: 2. Of those that a mesh axis runs over, the one named last changes fastest.
Arguments:
- tx_fields: bfloat16 [64, 32768], P(None, 'tile'), may hold values from -6 to 6
- rx_fields: bfloat16 [128, 32768], P(None, 'tile'), may hold values from -6 to 6
- layer_of_cell: int32 [32768], P('tile'), may hold values from 0 to 31
- layer_cond: float32 [32], replicated, may hold values from 0.05 to 5
- tx_of_row: int32 [2816], replicated, may hold values from 0 to 63
- rx_of_row: int32 [2816], replicated, may hold values from 0 to 127
- damping: float32 [2816], replicated, may hold values from 0.5 to 5
- panel_order: int32 [2816], replicated, may hold values from 0 to 2815, each once
Outputs:
- trailing: float32 [2816, 2816], P('grp', 'tile')
- factor: float32 [2816, 1024], P('grp')
The draws below stay inside these ranges and needn't reach their ends.
Inputs may be any that keep to these rules, and one draw needn't show every extreme that they name: `panel_order`: each data row appears exactly once; panel k is entries k * 512 to (k + 1) * 512 - 1.
All inputs are finite; a program needn't handle non-finite values.
Results may differ from the reference program's by a relative error of at most 0.0014.
Values may be sent and summed in bfloat16 or wider, within the bound.
A program may use at most 64 MiB of HBM per device.

```python
import math
import jax
import jax.numpy as jnp
from jax import lax

NC = 1024
PANEL = 512
NPAN = 2
NTX = 64
NRX = 128
NLAYER = 32
M = 2816
NCELLS = 32768


def touch_ends(drawn, stream_key, least, top_value):
    spot = [jax.random.randint(jax.random.fold_in(stream_key, axis), (), 0, length) for axis, length in enumerate(drawn.shape)]
    longest = drawn.shape.index(max(drawn.shape))
    neighbour = spot[:longest] + [(spot[longest] + 1) % drawn.shape[longest]] + spot[longest + 1:]
    return drawn.at[tuple(spot)].set(least).at[tuple(neighbour)].set(top_value)


def steps_of(rng, dims, cuts, smallest, largest):
    def one(axis_at, shards_of):
        steps = jax.random.uniform(jax.random.fold_in(jax.random.fold_in(rng, 6), axis_at), (shards_of,), jnp.float32, smallest / len(cuts), largest / len(cuts))
        return jnp.repeat(jnp.exp(steps), dims[axis_at] // shards_of).reshape((-1,) + (1,) * (len(dims) - axis_at - 1))

    gain = one(*cuts[0])
    for cut in cuts[1:]:
        gain = gain * one(*cut)
    return gain


def gaussian(rng, shape, width, bound, shards=(), dtype=jnp.bfloat16):
    entries = jax.random.normal(rng, shape, jnp.float32) * width
    if len(shards) > 0:
        entries = steps_of(rng, shape, shards, -0.22, 0.18) * entries
    return jnp.clip(entries, min=-bound, max=bound).astype(dtype)


def setup_inputs(seed: int = 0) -> dict:
    seeds = jax.random.split(jax.random.key(seed), 9)
    tx_fields = gaussian(seeds[0], (NTX, NCELLS), 1.0, 6.0, ((1, 32),))
    rx_fields = gaussian(seeds[1], (NRX, NCELLS), 1.0, 6.0, ((1, 32),))
    layer_of_cell = touch_ends(jax.random.randint(seeds[2], (NCELLS,), 0, NLAYER), jax.random.fold_in(seeds[2], 1), 0, NLAYER - 1).astype(jnp.int32)
    layer_cond = jnp.clip(jnp.exp(jax.random.uniform(seeds[3], (NLAYER,), jnp.float32, math.log(0.05), math.log(5.0))), 0.05, 5.0)
    tx_of_row = touch_ends(jax.random.randint(seeds[4], (M,), 0, NTX), jax.random.fold_in(seeds[4], 1), 0, NTX - 1).astype(jnp.int32)
    rx_of_row = touch_ends(jax.random.randint(seeds[5], (M,), 0, NRX), jax.random.fold_in(seeds[5], 1), 0, NRX - 1).astype(jnp.int32)
    damping = jnp.clip(jnp.exp(jax.random.uniform(seeds[6], (M,), jnp.float32, math.log(0.5), math.log(5.0))), 0.5, 5.0)
    panel_order = jax.random.permutation(seeds[7], M).astype(jnp.int32)
    return {"tx_fields": tx_fields, "rx_fields": rx_fields, "layer_of_cell": layer_of_cell, "layer_cond": layer_cond, "tx_of_row": tx_of_row, "rx_of_row": rx_of_row, "damping": damping, "panel_order": panel_order}


highest = lax.Precision.HIGHEST

def reference(tx_fields, rx_fields, layer_of_cell, layer_cond, tx_of_row, rx_of_row, damping, panel_order):
    cell_cond = jnp.take(layer_cond, layer_of_cell, axis=0)
    block_count = NCELLS // NC
    tx_blocks = tx_fields.reshape(NTX, block_count, NC).transpose(1, 0, 2)
    rx_blocks = rx_fields.reshape(NRX, block_count, NC).transpose(1, 0, 2)
    cond_blocks = cell_cond.reshape(block_count, NC)

    def add_block(gram, block_inputs):
        tx_block, rx_block, cond_block = block_inputs
        sens = jnp.take(tx_block, tx_of_row, axis=0).astype(jnp.float32) * jnp.take(rx_block, rx_of_row, axis=0).astype(jnp.float32) * cond_block[None, :]
        sens = sens.astype(jnp.bfloat16)
        return (gram + jnp.dot(sens.astype(jnp.float32), sens.T.astype(jnp.float32), preferred_element_type=jnp.float32), None)
    gram = jnp.zeros((M, M), jnp.float32)
    gram, unused = lax.scan(add_block, gram, (tx_blocks, rx_blocks, cond_blocks))
    gram = gram / NCELLS + jnp.diag(damping)
    factor_parts = []
    for turn_index in range(NPAN):
        chosen = panel_order[turn_index * PANEL:(turn_index + 1) * PANEL]
        panel_columns = jnp.take(gram, chosen, axis=1)
        diag_block = jnp.take(panel_columns, chosen, axis=0)
        block_factor = jnp.linalg.cholesky(diag_block)
        panel_factor = lax.linalg.triangular_solve(block_factor, panel_columns, left_side=False, lower=True, transpose_a=True)
        gram = gram - jnp.dot(panel_factor, panel_factor.T, precision=highest)
        factor_parts.append(panel_factor)
    return (gram, jnp.concatenate(factor_parts, axis=1))
```

```python
import functools

import jax
import jax.numpy as jnp
from jax import lax
from jax.experimental import pallas as pl
from jax.experimental.pallas import tpu as pltpu
from jax.sharding import PartitionSpec as P

F32 = jnp.float32
BF16 = jnp.bfloat16
MESH = pl.DeviceIdType.MESH
VMEM = pltpu.VMEM
DMA = pltpu.SemaphoreType.DMA

M = 2816
NCELLS = 32768
PICKED = 1024
NX, NY, NZ, NCORE = 4, 4, 8, 2
NG = NX * NCORE
NT = NY * NZ
ROWS = M // NG
COLS = M // NT
PG = PICKED // NG
PT = PICKED // NT
CELLS = NCELLS // NT
RIGHT = 512
LEFT = COLS + PT
B = 128


def dot(a, b, ca, cb):
    return lax.dot_general(a, b, (((ca,), (cb,)), ((), ())), preferred_element_type=F32)


def split(x):
    hi = x.astype(BF16)
    return hi, (x - hi.astype(F32)).astype(BF16)


def places():
    g = lax.axis_index("grp")
    t = lax.axis_index("tile")
    return g // NCORE, g % NCORE, t // NY, t % NY


def at_z(z, y):
    return {"tile": lax.rem(z + NZ, NZ) * NY + y}


def greet(peers):
    barrier = pltpu.get_barrier_semaphore()
    for peer in peers:
        pl.semaphore_signal(barrier, inc=1, device_id=peer, device_id_type=MESH)
    pl.semaphore_wait(barrier, len(peers))


def sends(src, dst, send, recv, peer):
    return pltpu.make_async_remote_copy(
        src_ref=src, dst_ref=dst, send_sem=send, recv_sem=recv, device_id=peer, device_id_type=MESH
    )


def owner_of(z, i):
    hops = (i + 1) // 2
    return lax.rem(z + NZ + jnp.where(i % 2 == 1, -hops, hops), NZ)


def gram_kernel(
    fields_ref, cond_ref, tx_hot_ref, rx_hot_ref, out_ref, held, conds, sens,
    ring_send, ring_recv, cond_send, cond_recv, pair_send, pair_recv, local,
):
    x, c, z, y = places()
    up, down, pair = at_z(z + 1, y), at_z(z + NZ - 1, y), {"grp": x * NCORE + 1 - c}
    greet((up, down, pair))

    def ring(i, peer, first):
        o = z if first else owner_of(z, i - 2)
        half = fields_ref.at[c] if first else held.at[o, c]
        line = cond_ref if first else conds.at[o]
        return (
            sends(half, held.at[o, c], ring_send.at[i], ring_recv.at[i], peer),
            sends(line, conds.at[o], cond_send.at[i], cond_recv.at[i], peer),
        )

    def to_pair(i):
        o = owner_of(z, i)
        return sends(held.at[o, c], held.at[o, c], pair_send.at[i], pair_recv.at[i], pair)

    def start(copies):
        for copy in copies:
            copy.start()

    start(ring(1, up, True))
    start(ring(2, down, True))
    mine = pltpu.make_async_copy(fields_ref, held.at[z], local.at[0])
    mine_line = pltpu.make_async_copy(cond_ref, conds.at[z], local.at[1])
    mine.start()
    mine_line.start()
    out_ref[...] = jnp.zeros_like(out_ref)
    mine.wait()
    mine_line.wait()

    def arrive(i, peer, onward):
        for copy in ring(i, peer, False):
            copy.wait_recv()
        to_pair(i).start()
        if onward is not None:
            start(ring(i + 2, onward, False))

    def body(i, carry):
        @pl.when((i % 2 == 1) & (i < 6))
        def _():
            for copy in ring(i + 2, up, False):
                copy.wait_recv()
            to_pair(i + 2).start()

        @pl.when((i % 2 == 1) & (i < 4))
        def _():
            start(ring(i + 4, up, False))

        @pl.when((i % 2 == 0) & (i < 6))
        def _():
            for copy in ring(i + 2, down, False):
                copy.wait_recv()
            to_pair(i + 2).start()

        @pl.when((i % 2 == 0) & (i < 4))
        def _():
            start(ring(i + 4, down, False))

        @pl.when(i >= 1)
        def _():
            to_pair(i).wait_recv()

        o = owner_of(z, i)
        width = 256

        def chunk(j, carry):
            at = pl.ds(pl.multiple_of(j * width, width), width)
            txs = held[o, 0, 0:64, at]
            rxs = jnp.concatenate([held[o, 0, 64:96, at], held[o, 1, :, at]], axis=0)
            part = dot(tx_hot_ref[...], txs, 1, 0) * dot(rx_hot_ref[...], rxs, 1, 0)
            sens[:, at] = (part * conds[o, :, at]).astype(BF16)
            return carry

        lax.fori_loop(0, CELLS // width, chunk, 0)
        out_ref[...] += dot(sens[RIGHT:, :], sens[0:RIGHT, :], 1, 1)
        return carry

    for copy in ring(1, up, True):
        copy.wait_recv()
    to_pair(1).start()
    start(ring(3, up, False))
    lax.fori_loop(0, NZ, body, 0)

    for i in range(1, NZ):
        for copy in ring(i, up if i % 2 == 1 else down, i < 3):
            copy.wait_send()
        to_pair(i).wait_send()


def gram_sums(fields, cond, tx_hot, rx_hot):
    vmem = pl.BlockSpec(memory_space=VMEM)
    return pl.pallas_call(
        gram_kernel,
        out_shape=jax.ShapeDtypeStruct((NY * LEFT, RIGHT), F32),
        in_specs=[vmem] * 4,
        out_specs=vmem,
        scratch_shapes=[
            VMEM((NZ, NCORE, 96, CELLS), BF16),
            VMEM((NZ, 1, CELLS), F32),
            VMEM((RIGHT + NY * LEFT, CELLS), BF16),
        ]
        + [DMA((NZ,))] * 6
        + [DMA((2,))],
        compiler_params=pltpu.CompilerParams(
            collective_id=0, has_side_effects=True, vmem_limit_bytes=40 << 20
        ),
        name="gram_sums",
    )(fields, cond, tx_hot, rx_hot)


def spread_kernel(
    part_ref, damp_ref, own_ref, rows_ref, diag_ref, cross_ref, got, own,
    sum_send, sum_recv, y_send, y_recv, ring_send, ring_recv,
    x_send, x_recv, pair_send, pair_recv, ex_send, ex_recv, ep_send, ep_recv, local,
):
    x, c, z, y = places()
    g = x * NCORE + c
    up, down, pair = at_z(z + 1, y), at_z(z + NZ - 1, y), {"grp": x * NCORE + 1 - c}
    at_y = [None] + [{"tile": z * NY + lax.rem(y + d, NY)} for d in range(1, NY)]
    at_x = [None] + [{"grp": lax.rem(x + d, NX) * NCORE + c} for d in range(1, NX)]
    greet(at_y[1:] + at_x[1:] + [up, down, pair])

    sums = [
        sends(part_ref.at[lax.rem(y + d, NY)], got.at[d], sum_send.at[d], sum_recv.at[d], at_y[d])
        for d in range(1, NY)
    ]
    for copy in sums:
        copy.start()
    total = part_ref[y]
    for d, copy in enumerate(sums, 1):
        copy.wait_recv()
        total += got[d]
    own[...] = total * (1.0 / NCELLS) + damp_ref[...]

    picked = own.at[COLS:LEFT, :]
    crossed = own.at[0:COLS, 0:PG]
    ys = [sends(picked, rows_ref.at[z, y], y_send.at[d], y_recv.at[d], at_y[d]) for d in range(1, NY)]
    for copy in ys:
        copy.start()
    mine = [
        pltpu.make_async_copy(picked, rows_ref.at[z, y], local.at[0]),
        pltpu.make_async_copy(crossed, cross_ref.at[g], local.at[1]),
        pltpu.make_async_copy(own, own_ref, local.at[2]),
    ]
    for copy in mine:
        copy.start()
    exs = [sends(crossed, cross_ref.at[g], ex_send.at[d], ex_recv.at[d], at_x[d]) for d in range(1, NX)]
    eps = [sends(crossed, cross_ref.at[g], ep_send.at[0], ep_recv.at[0], pair)]
    for copy in exs + eps:
        copy.start()
    mine[0].wait()
    for copy in ys:
        copy.wait_recv()

    def ring(i, peer):
        o = owner_of(z, i - 2) if i > 2 else z
        return sends(rows_ref.at[o], rows_ref.at[o], ring_send.at[i], ring_recv.at[i], peer)

    def g_from(d):
        return lax.rem(x + NX - d, NX) * NCORE + c

    def across(i, d):
        o = owner_of(z, i)
        return sends(
            rows_ref.at[o, :, :, 0:PG], diag_ref.at[g, o], x_send.at[d, i], x_recv.at[d, i], at_x[d]
        )

    def to_pair(i, d):
        o = owner_of(z, i)
        if d == 0:
            return sends(
                rows_ref.at[o, :, :, 0:PG], diag_ref.at[g, o], pair_send.at[d, i], pair_recv.at[d, i], pair
            )
        gd = g_from(d)
        return sends(diag_ref.at[gd, o], diag_ref.at[gd, o], pair_send.at[d, i], pair_recv.at[d, i], pair)

    def keep(i):
        o = owner_of(z, i)
        return pltpu.make_async_copy(rows_ref.at[o, :, :, 0:PG], diag_ref.at[g, o], local.at[3 + i])

    def relay(i):
        for d in range(1, NX):
            across(i, d).wait_recv()
            to_pair(i, d).start()

    ring(1, up).start()
    ring(2, down).start()
    for i in range(NZ):
        if i > 0:
            ring(i, up if i % 2 == 1 else down).wait_recv()
            if i + 2 < NZ:
                ring(i + 2, up if i % 2 == 1 else down).start()
        for d in range(1, NX):
            across(i, d).start()
        to_pair(i, 0).start()
        keep(i).start()
        if i > 1:
            relay(i - 2)
    for d, copy in enumerate(exs, 1):
        copy.wait_recv()
        gd = g_from(d)
        eps.append(sends(cross_ref.at[gd], cross_ref.at[gd], ep_send.at[d], ep_recv.at[d], pair))
        eps[-1].start()
    relay(NZ - 2)
    relay(NZ - 1)

    for i in range(NZ):
        keep(i).wait()
        for d in range(NX):
            to_pair(i, d).wait_recv()
            to_pair(i, d).wait_send()
        for d in range(1, NX):
            across(i, d).wait_send()
        if i > 0:
            ring(i, up if i % 2 == 1 else down).wait_send()
    for copy in eps:
        copy.wait_recv()
        copy.wait_send()
    for copy in sums + ys + exs:
        copy.wait_send()
    mine[1].wait()
    mine[2].wait()


def spread(part, damp):
    vmem = pl.BlockSpec(memory_space=VMEM)
    return pl.pallas_call(
        spread_kernel,
        out_shape=(
            jax.ShapeDtypeStruct((LEFT, RIGHT), F32),
            jax.ShapeDtypeStruct((NZ, NY, PT, RIGHT), F32),
            jax.ShapeDtypeStruct((NG, NZ, NY, PT, PG), F32),
            jax.ShapeDtypeStruct((NG, COLS, PG), F32),
        ),
        in_specs=[vmem] * 2,
        out_specs=(vmem,) * 4,
        scratch_shapes=[VMEM((NY, LEFT, RIGHT), F32), VMEM((LEFT, RIGHT), F32)]
        + [DMA((NY,))] * 4
        + [DMA((NZ,))] * 2
        + [DMA((NX, NZ))] * 4
        + [DMA((NX,))] * 4
        + [DMA((3 + NZ,))],
        compiler_params=pltpu.CompilerParams(
            collective_id=1, has_side_effects=True, vmem_limit_bytes=40 << 20
        ),
        name="spread",
    )(part, damp)


def inverse_factor(m):
    lane = lax.broadcasted_iota(jnp.int32, (8, B), 1)
    sub = lax.broadcasted_iota(jnp.int32, (8, B), 0)
    tiles = [m[8 * i : 8 * i + 8, :] for i in range(B // 8)]
    full = lambda v: jnp.broadcast_to(v, (8, B))
    column = lambda t, j: jnp.take_along_axis(t, jnp.full((8, B), j, jnp.int32), axis=1)
    for j in range(0, B, 4):
        q, s = divmod(j, 8)
        t = tiles[q]
        cs = [column(t, j + p) for p in range(4)]
        here = (lane >= j) & (lane < j + 4)
        rows = []
        for p in range(4):
            row = jnp.where(here, 0.0, full(t[s + p : s + p + 1, :]))
            rows.append(jnp.where(lane == j + p, 1.0, row))
        low, root, solved = {}, [], []
        for p in range(4):
            pivot = full(cs[p][s + p : s + p + 1, :])
            for k in range(p):
                pivot = pivot - low[p, k] * low[p, k]
            root.append(lax.rsqrt(pivot))
            for i in range(p + 1, 4):
                v = full(cs[p][s + i : s + i + 1, :])
                for k in range(p):
                    v = v - low[i, k] * low[p, k]
                low[i, p] = v * root[p]
            v = rows[p]
            for k in range(p):
                v = v - low[p, k] * solved[k]
            solved.append(v * root[p])
        back = [None] * 4
        for p in reversed(range(4)):
            v = solved[p]
            for i in range(p + 1, 4):
                v = v - low[i, p] * back[i]
            back[p] = v * root[p]
        for i in range(q, B // 8):
            new = t if i == q else tiles[i]
            if i > q or s == 0:
                zs = [column(new, j + p) for p in range(4)]
                new = jnp.where(here, 0.0, new)
                for p in range(4):
                    new = new - zs[p] * back[p]
            if i == q:
                new = jnp.where(sub >= s + 4, new, t)
                for p in range(4):
                    new = jnp.where(sub == s + p, solved[p], new)
            tiles[i] = new
    w = jnp.concatenate(tiles, axis=0)
    r = lax.broadcasted_iota(jnp.int32, (B, B), 0)
    c = lax.broadcasted_iota(jnp.int32, (B, B), 1)
    return jnp.where(r >= c, w, 0.0)


GC = RIGHT - PG
WIDE = PICKED + GC + B


def solve_kernel(own_ref, rows_ref, diag_ref, cross_ref, trail_ref, factor_ref, acc, high, low):
    def block(k, carry):
        at = pl.ds(pl.multiple_of(k * B, B), B)
        for g in range(NG):
            acc[:, g * B : (g + 1) * B] = diag_ref[g, at, :]
        acc[:, PICKED : PICKED + GC] = rows_ref[at, PG:RIGHT]
        padded = jnp.concatenate([cross_ref[k], jnp.zeros((B - COLS, B), F32)], axis=0)
        acc[:, PICKED + GC :] = padded.T

        def before(j, carry):
            prior = pl.ds(pl.multiple_of(j * B, B), B)
            lh, ll = high[prior, at], low[prior, at]
            rh, rl = high[prior, :], low[prior, :]
            acc[...] -= dot(lh, rh, 0, 0) + (dot(lh, rl, 0, 0) + dot(ll, rh, 0, 0))
            return carry

        lax.fori_loop(0, k, before, 0)
        wh, wl = split(inverse_factor(acc[:, at]))
        ah, al = split(acc[...])
        u = dot(wh, ah, 1, 0) + (dot(wh, al, 1, 0) + dot(wl, ah, 1, 0))
        uh, ul = split(u)
        high[at, :] = uh
        low[at, :] = ul
        factor_ref[:, at] = u[:, PICKED : PICKED + GC].T[0:ROWS, :]
        return carry

    lax.fori_loop(0, NG, block, 0)
    gh, gl = high[:, PICKED : PICKED + GC], low[:, PICKED : PICKED + GC]
    th, tl = high[:, PICKED + GC :], low[:, PICKED + GC :]
    drop = dot(gh, th, 0, 0) + (dot(gh, tl, 0, 0) + dot(gl, th, 0, 0))
    gram = jnp.concatenate([own_ref[0:COLS, PG:RIGHT], jnp.zeros((B - COLS, GC), F32)], axis=0)
    trail_ref[...] = (gram.T - drop)[0:ROWS, 0:COLS]


def solve(own, rows, diag, cross):
    vmem = pl.BlockSpec(memory_space=VMEM)
    return pl.pallas_call(
        solve_kernel,
        out_shape=(
            jax.ShapeDtypeStruct((ROWS, COLS), F32),
            jax.ShapeDtypeStruct((ROWS, PICKED), F32),
        ),
        in_specs=[vmem] * 4,
        out_specs=(vmem, vmem),
        scratch_shapes=[VMEM((B, WIDE), F32), VMEM((PICKED, WIDE), BF16), VMEM((PICKED, WIDE), BF16)],
        compiler_params=pltpu.CompilerParams(vmem_limit_bytes=40 << 20),
        name="solve",
    )(own, rows, diag, cross)


def shards(
    tx_fields, rx_fields, layer_of_cell, layer_cond, tx_of_row, rx_of_row, damping, panel_order
):
    g = lax.axis_index("grp")
    t = lax.axis_index("tile")
    z, y = t // NY, t % NY
    levels = jnp.arange(layer_cond.shape[0], dtype=jnp.int32)
    hit = levels[:, None] == layer_of_cell[None, :]
    cond = jnp.sum(jnp.where(hit, layer_cond[:, None], 0.0), axis=0, keepdims=True)
    fields = jnp.concatenate([tx_fields, rx_fields], axis=0).reshape(2, 96, CELLS)

    pair_of_row = tx_of_row * 128 + rx_of_row
    picks = jnp.concatenate(
        [
            lax.dynamic_slice_in_dim(panel_order, g * PG, PG),
            lax.dynamic_slice_in_dim(panel_order, z * (PT * NY), PT * NY),
        ]
    )
    chosen = picks[:, None] == jnp.arange(M, dtype=jnp.int32)[None, :]
    pair_picks = jnp.sum(jnp.where(chosen, pair_of_row[None, :], 0), axis=1)
    damp_picks = jnp.sum(jnp.where(chosen, damping[None, :], 0.0), axis=1)
    right = [
        pair_picks[:PG],
        lax.dynamic_slice_in_dim(pair_of_row, g * ROWS, ROWS),
        jnp.full((RIGHT - PG - ROWS,), -1, jnp.int32),
    ]
    near = lax.dynamic_slice_in_dim(pair_of_row, z * (COLS * NY), COLS * NY).reshape(NY, COLS)
    left = jnp.concatenate([near, pair_picks[PG:].reshape(NY, PT)], axis=1).reshape(-1)
    pairs = jnp.concatenate(right + [left])[:, None]
    tx_hot = (pairs // 128 == jnp.arange(64)[None, :]).astype(BF16)
    rx_hot = ((pairs % 128 == jnp.arange(128)[None, :]) & (pairs >= 0)).astype(BF16)

    left_ids = jnp.concatenate(
        [t * COLS + jnp.arange(COLS), lax.dynamic_slice_in_dim(picks, PG + y * PT, PT)]
    )
    right_ids = jnp.concatenate(
        [picks[:PG], g * ROWS + jnp.arange(ROWS), jnp.full((RIGHT - PG - ROWS,), -1)]
    )
    left_damp = jnp.concatenate(
        [
            lax.dynamic_slice_in_dim(damping, t * COLS, COLS),
            lax.dynamic_slice_in_dim(damp_picks, PG + y * PT, PT),
        ]
    )
    damp = jnp.where(left_ids[:, None] == right_ids[None, :], left_damp[:, None], 0.0)

    part = gram_sums(fields, cond, tx_hot, rx_hot)
    own, rows, diag, cross = spread(part.reshape(NY, LEFT, RIGHT), damp)
    return solve(
        own, rows.reshape(PICKED, RIGHT), diag.reshape(NG, PICKED, PG), cross
    )


def solution(mesh):
    placed = (P(None, "tile"), P(None, "tile"), P("tile"), P(), P(), P(), P(), P())
    return jax.shard_map(
        shards,
        mesh=mesh,
        in_specs=placed,
        out_specs=(P("grp", "tile"), P("grp", None)),
        check_vma=False,
    )
```

```python
import functools

import jax
import jax.numpy as jnp
from jax import lax
from jax.experimental import pallas as pl
from jax.experimental.pallas import tpu as pltpu
from jax.sharding import PartitionSpec as P

F32 = jnp.float32
BF16 = jnp.bfloat16
MESH = pl.DeviceIdType.MESH
VMEM = pltpu.VMEM
DMA = pltpu.SemaphoreType.DMA

M = 2816
NCELLS = 32768
PICKED = 1024
NX, NY, NZ, NCORE = 4, 4, 8, 2
NG = NX * NCORE
NT = NY * NZ
ROWS = M // NG
COLS = M // NT
PG = PICKED // NG
PT = PICKED // NT
CELLS = NCELLS // NT
RIGHT = 512
LEFT = COLS + PT
B = 128


def dot(a, b, ca, cb):
    return lax.dot_general(a, b, (((ca,), (cb,)), ((), ())), preferred_element_type=F32)


def split(x):
    hi = x.astype(BF16)
    return hi, (x - hi.astype(F32)).astype(BF16)


def places():
    g = lax.axis_index("grp")
    t = lax.axis_index("tile")
    return g // NCORE, g % NCORE, t // NY, t % NY


def at_z(z, y):
    return {"tile": lax.rem(z + NZ, NZ) * NY + y}


def greet(peers):
    barrier = pltpu.get_barrier_semaphore()
    for peer in peers:
        pl.semaphore_signal(barrier, inc=1, device_id=peer, device_id_type=MESH)
    pl.semaphore_wait(barrier, len(peers))


def sends(src, dst, send, recv, peer):
    return pltpu.make_async_remote_copy(
        src_ref=src, dst_ref=dst, send_sem=send, recv_sem=recv, device_id=peer, device_id_type=MESH
    )


def owner_of(z, i):
    hops = (i + 1) // 2
    return lax.rem(z + NZ + jnp.where(i % 2 == 1, -hops, hops), NZ)


def gram_kernel(
    fields_ref, cond_ref, tx_hot_ref, rx_hot_ref, out_ref, held, conds, sens,
    ring_send, ring_recv, cond_send, cond_recv, pair_send, pair_recv, local,
):
    x, c, z, y = places()
    up, down, pair = at_z(z + 1, y), at_z(z + NZ - 1, y), {"grp": x * NCORE + 1 - c}
    greet((up, down, pair))

    def ring(i, peer, first):
        o = z if first else owner_of(z, i - 2)
        half = fields_ref.at[c] if first else held.at[o, c]
        line = cond_ref if first else conds.at[o]
        return (
            sends(half, held.at[o, c], ring_send.at[i], ring_recv.at[i], peer),
            sends(line, conds.at[o], cond_send.at[i], cond_recv.at[i], peer),
        )

    def to_pair(i):
        o = owner_of(z, i)
        return sends(held.at[o, c], held.at[o, c], pair_send.at[i], pair_recv.at[i], pair)

    def start(copies):
        for copy in copies:
            copy.start()

    start(ring(1, up, True))
    start(ring(2, down, True))
    mine = pltpu.make_async_copy(fields_ref, held.at[z], local.at[0])
    mine_line = pltpu.make_async_copy(cond_ref, conds.at[z], local.at[1])
    mine.start()
    mine_line.start()
    out_ref[...] = jnp.zeros_like(out_ref)
    mine.wait()
    mine_line.wait()

    def arrive(i, peer, onward):
        for copy in ring(i, peer, False):
            copy.wait_recv()
        to_pair(i).start()
        if onward is not None:
            start(ring(i + 2, onward, False))

    def body(i, carry):
        @pl.when((i % 2 == 1) & (i < 6))
        def _():
            for copy in ring(i + 2, up, False):
                copy.wait_recv()
            to_pair(i + 2).start()

        @pl.when((i % 2 == 1) & (i < 4))
        def _():
            start(ring(i + 4, up, False))

        @pl.when((i % 2 == 0) & (i < 6))
        def _():
            for copy in ring(i + 2, down, False):
                copy.wait_recv()
            to_pair(i + 2).start()

        @pl.when((i % 2 == 0) & (i < 4))
        def _():
            start(ring(i + 4, down, False))

        @pl.when(i >= 1)
        def _():
            to_pair(i).wait_recv()

        o = owner_of(z, i)
        width = 256

        def chunk(j, carry):
            at = pl.ds(pl.multiple_of(j * width, width), width)
            txs = held[o, 0, 0:64, at]
            rxs = jnp.concatenate([held[o, 0, 64:96, at], held[o, 1, :, at]], axis=0)
            part = dot(tx_hot_ref[...], txs, 1, 0) * dot(rx_hot_ref[...], rxs, 1, 0)
            sens[:, at] = (part * conds[o, :, at]).astype(BF16)
            return carry

        lax.fori_loop(0, CELLS // width, chunk, 0)
        out_ref[...] += dot(sens[RIGHT:, :], sens[0:RIGHT, :], 1, 1)
        return carry

    for copy in ring(1, up, True):
        copy.wait_recv()
    to_pair(1).start()
    start(ring(3, up, False))
    lax.fori_loop(0, NZ, body, 0)

    for i in range(1, NZ):
        for copy in ring(i, up if i % 2 == 1 else down, i < 3):
            copy.wait_send()
        to_pair(i).wait_send()


def gram_sums(fields, cond, tx_hot, rx_hot):
    vmem = pl.BlockSpec(memory_space=VMEM)
    return pl.pallas_call(
        gram_kernel,
        out_shape=jax.ShapeDtypeStruct((NY * LEFT, RIGHT), F32),
        in_specs=[vmem] * 4,
        out_specs=vmem,
        scratch_shapes=[
            VMEM((NZ, NCORE, 96, CELLS), BF16),
            VMEM((NZ, 1, CELLS), F32),
            VMEM((RIGHT + NY * LEFT, CELLS), BF16),
        ]
        + [DMA((NZ,))] * 6
        + [DMA((2,))],
        compiler_params=pltpu.CompilerParams(
            collective_id=0, has_side_effects=True, vmem_limit_bytes=40 << 20
        ),
        name="gram_sums",
    )(fields, cond, tx_hot, rx_hot)


def tree(vs):
    while len(vs) > 1:
        vs = [vs[i] + vs[i + 1] if i + 1 < len(vs) else vs[i] for i in range(0, len(vs), 2)]
    return vs[0]


def inverse_factor(m):
    W = 16
    H = W // 8
    lane = lax.broadcasted_iota(jnp.int32, (8, B), 1)
    sub = lax.broadcasted_iota(jnp.int32, (8, B), 0)
    tiles = [m[8 * i : 8 * i + 8, :] for i in range(B // 8)]
    full = lambda v: jnp.broadcast_to(v, (8, B))
    column = lambda t, j: jnp.take_along_axis(t, jnp.full((8, B), j, jnp.int32), axis=1)
    for j in range(0, B, W):
        q = j // 8
        here = (lane >= j) & (lane < j + W)
        cs = {}
        for p in range(W):
            for h in range(p // 8, H):
                cs[p, h] = column(tiles[q + h], j + p)
        rows = [
            jnp.where(lane == j + 8 * h + sub, 1.0, jnp.where(here, 0.0, tiles[q + h])) for h in range(H)
        ]
        pivots, inverses, solved, low = [], [], [], {}
        for p in range(W):
            hp, s = divmod(p, 8)
            pivot = full(cs[p, hp][s : s + 1, :])
            inverse = 1.0 / pivot
            pivots.append(pivot)
            inverses.append(inverse)
            row = full(rows[hp][s : s + 1, :])
            solved.append(row)
            for k in range(p + 1, W):
                low[k, p] = full(cs[p, k // 8][k % 8 : k % 8 + 1, :]) * inverse
                for h in range(k // 8, H):
                    cs[k, h] = cs[k, h] - cs[p, h] * low[k, p]
            scaled = row * inverse
            for h in range(hp, H):
                if h == hp and s == 7:
                    continue
                f = jnp.where(sub > s, cs[p, h], 0.0) if h == hp else cs[p, h]
                rows[h] = rows[h] - f * scaled
        back = [None] * W
        for p in reversed(range(W)):
            v = solved[p] * inverses[p]
            for i in reversed(range(p + 1, W)):
                v = v - low[i, p] * back[i]
            back[p] = v
        for i in range(q + H, B // 8):
            terms = [column(tiles[i], j + p) * back[p] for p in range(W)]
            tiles[i] = jnp.where(here, 0.0, tiles[i]) - tree(terms)
        for h in range(H):
            scale = pivots[8 * h]
            for s in range(1, 8):
                scale = jnp.where(sub == s, pivots[8 * h + s], scale)
            tiles[q + h] = rows[h] * lax.rsqrt(scale)
    w = jnp.concatenate(tiles, axis=0)
    r = lax.broadcasted_iota(jnp.int32, (B, B), 0)
    c = lax.broadcasted_iota(jnp.int32, (B, B), 1)
    return jnp.where(r >= c, w, 0.0)


GC = RIGHT - PG
SIDE = GC + B


def dot3(ah, al, bh, bl, ca, cb):
    return dot(ah, bh, ca, cb) + (dot(ah, bl, ca, cb) + dot(al, bh, ca, cb))


def block_of(k):
    return pl.ds(pl.multiple_of(k * B, B), B)


DIAG, PICK, CROSS, REST = 0, 1, 2, 3
PARTS = (
    (slice(COLS, LEFT), slice(0, PG)),
    (slice(COLS, LEFT), slice(PG, RIGHT)),
    (slice(0, COLS), slice(0, PG)),
    (slice(0, COLS), slice(PG, RIGHT)),
)


def solve_kernel(
    part_ref, damp_ref, trail_ref, factor_ref,
    now, acc, nxt, high, low, wh, wl, xh, xl, got, diag, side_rows, cross, rest,
    rs_send, rs_recv, dz_send, dz_recv, dy_send, dy_recv, dx_send, dx_recv, dp_send, dp_recv,
    cz_send, cz_recv, cy_send, cy_recv, ex_send, ex_recv, ep_send, ep_recv,
):
    x, c, z, y = places()
    g = x * NCORE + c
    pair = {"grp": x * NCORE + 1 - c}
    at_y = [None] + [{"tile": z * NY + lax.rem(y + d, NY)} for d in range(1, NY)]
    at_x = [None] + [{"grp": lax.rem(x + d, NX) * NCORE + c} for d in range(1, NX)]
    in_z = [None] + [{"tile": lax.rem(z + d, NZ) * NY + y} for d in range(1, NZ)]
    greet(at_y[1:] + at_x[1:] + in_z[1:] + [pair])

    def rs(p, d):
        rows, cols = PARTS[p]
        return sends(
            part_ref.at[lax.rem(y + d, NY), rows, cols], got.at[d - 1, rows, cols],
            rs_send.at[p, d], rs_recv.at[p, d], at_y[d],
        )

    def start_sums(p):
        for d in range(1, NY):
            rs(p, d).start()

    def summed(p):
        rows, cols = PARTS[p]
        total = part_ref[y, rows, cols]
        for d in range(1, NY):
            rs(p, d).wait_recv()
            total += got[d - 1, rows, cols]
        return total * (1.0 / NCELLS) + damp_ref[rows, cols]

    def dz(d):
        return sends(diag.at[g, z, y], diag.at[g, z, y], dz_send.at[d], dz_recv.at[d], in_z[d])

    def dy(zz, d):
        return sends(diag.at[g, zz, y], diag.at[g, zz, y], dy_send.at[zz, d], dy_recv.at[zz, d], at_y[d])

    def dx(zz, d):
        return sends(diag.at[g, zz], diag.at[g, zz], dx_send.at[zz, d], dx_recv.at[zz, d], at_x[d])

    def dp(zz, d):
        gd = lax.rem(x + NX - d, NX) * NCORE + c
        return sends(diag.at[gd, zz], diag.at[gd, zz], dp_send.at[zz, d], dp_recv.at[zz, d], pair)

    def cz(d):
        return sends(side_rows.at[z, y], side_rows.at[z, y], cz_send.at[d], cz_recv.at[d], in_z[d])

    def cy(zz, d):
        return sends(side_rows.at[zz, y], side_rows.at[zz, y], cy_send.at[zz, d], cy_recv.at[zz, d], at_y[d])

    def ex(d):
        return sends(cross.at[g], cross.at[g], ex_send.at[d], ex_recv.at[d], at_x[d])

    def ep(d):
        gd = lax.rem(x + NX - d, NX) * NCORE + c
        return sends(cross.at[gd], cross.at[gd], ep_send.at[d], ep_recv.at[d], pair)

    def arrived(zz, copy, sem_recv, ref):
        d = lax.rem(z + NZ - zz, NZ)

        @pl.when(d != 0)
        def _():
            sends(ref.at[zz, y], ref.at[zz, y], sem_recv.at[d], sem_recv.at[d], pair).wait_recv()

    def across(zz):
        for d in range(1, NX):
            dx(zz, d).wait_recv()
            dp(zz, d).start()

    def complete(zz):
        for d in range(NX):
            dp(zz, d).wait_recv()

    start_sums(DIAG)
    high[...] = jnp.zeros_like(high)
    low[...] = jnp.zeros_like(low)
    xh[...] = jnp.zeros_like(xh)
    xl[...] = jnp.zeros_like(xl)
    acc[...] = jnp.zeros_like(acc)
    wh[0] = jnp.zeros((B, B), BF16)
    wl[0] = jnp.zeros((B, B), BF16)
    diag[g, z, y] = summed(DIAG)
    for d in range(1, NZ):
        dz(d).start()
    start_sums(PICK)
    for zz in range(NZ):
        arrived(zz, None, dz_recv, diag.at[g])
        for d in range(1, NY):
            dy(zz, d).start()
    start_sums(CROSS)
    for zz in range(NZ):
        for d in range(1, NY):
            dy(zz, d).wait_recv()
        for d in range(1, NX):
            dx(zz, d).start()
        dp(zz, 0).start()
    start_sums(REST)
    across(0)
    across(1)
    complete(0)

    def diag_rows(k, begin):
        return jnp.concatenate([diag[i, k].reshape(B, B) for i in range(begin, NG)], axis=1)

    nxt[...] = diag_rows(0, 0)
    now[...] = diag[0, 0].reshape(B, B)

    def block(k, begin, depth):
        w = inverse_factor(now[...])
        last = jnp.maximum(k - 1, 0)
        cols = slice(begin * B, PICKED)
        ah, al = split(acc[:, cols])
        uh, ul = split(dot3(wh[last], wl[last], ah, al, 1, 0))
        high[block_of(last), cols] = uh
        low[block_of(last), cols] = ul
        at = block_of(k)
        acc[:, cols] = nxt[:, cols] - dot3(high[block_of(last), at], low[block_of(last), at], uh, ul, 0, 0)
        after = jnp.minimum(k + 1, NG - 1)
        there = block_of(after)
        nxt[:, cols] = diag_rows(after, begin) - dot3(
            high[0:depth, there], low[0:depth, there], high[0:depth, cols], low[0:depth, cols], 0, 0
        )
        nh, nl = split(w)
        wh[k] = nh
        wl[k] = nl
        bh, bl = split(acc[:, there])
        vh, vl = split(dot3(nh, nl, bh, bl, 1, 0))
        now[...] = nxt[:, there] - dot3(vh, vl, vh, vl, 0, 0)

    def side(i, depth):
        at = block_of(i)
        padded = jnp.concatenate([cross[i], jnp.zeros((B - COLS, B), F32)], axis=0).T
        start = jnp.concatenate([side_rows[i].reshape(B, GC), padded], axis=1)
        done = dot3(high[0:depth, at], low[0:depth, at], xh[0:depth, :], xl[0:depth, :], 0, 0)
        sh, sl = split(start - done)
        u = dot3(wh[i], wl[i], sh, sl, 1, 0)
        uh, ul = split(u)
        xh[at, :] = uh
        xl[at, :] = ul
        factor_ref[:, at] = u[:, 0:GC].T[0:ROWS, :]

    def first(k, carry):
        across(k + 2)
        complete(k + 1)

        @pl.when(k == 0)
        def _():
            side_rows[z, y] = summed(PICK)
            for d in range(1, NZ):
                cz(d).start()
            cross[g] = summed(CROSS)
            for d in range(1, NX):
                ex(d).start()
            ep(0).start()

        @pl.when(k == 2)
        def _():
            for zz in range(NZ):
                arrived(zz, None, cz_recv, side_rows)
                for d in range(1, NY):
                    cy(zz, d).start()
            for d in range(1, NX):
                ex(d).wait_recv()
                ep(d).start()

        block(k, 0, 4 * B)
        return carry

    def here(i):
        for d in range(1, NY):
            cy(i, d).wait_recv()

    def second(k, carry):
        across(k + 2)
        complete(k + 1)
        i = 2 * (k - 4)
        here(i)
        here(i + 1)
        block(k, 3, 5 * B)
        side(i, 4 * B)
        side(i + 1, 4 * B)
        return carry

    def third(k, carry):
        @pl.when(k < NG - 1)
        def _():
            complete(k + 1)

        here(k - 2)
        block(k, 5, 7 * B)
        side(k - 2, 6 * B)
        return carry

    lax.fori_loop(0, 4, first, 0)
    for d in range(NX):
        ep(d).wait_recv()
    lax.fori_loop(4, 6, second, 0)
    lax.fori_loop(6, NG, third, 0)
    here(NG - 2)
    here(NG - 1)
    side(NG - 2, 6 * B)
    side(NG - 1, 7 * B)
    rest[0:COLS, :] = summed(REST)
    rest[COLS:, :] = jnp.zeros((B - COLS, GC), F32)
    drop = dot3(xh[:, 0:GC], xl[:, 0:GC], xh[:, GC:], xl[:, GC:], 0, 0)
    trail_ref[...] = (rest[...].T - drop)[0:ROWS, 0:COLS]

    for d in range(1, NY):
        for p in range(4):
            rs(p, d).wait_send()
        for zz in range(NZ):
            dy(zz, d).wait_send()
            cy(zz, d).wait_send()
    for d in range(1, NZ):
        dz(d).wait_send()
        cz(d).wait_send()
    for d in range(NX):
        for zz in range(NZ):
            if d:
                dx(zz, d).wait_send()
            dp(zz, d).wait_send()
        if d:
            ex(d).wait_send()
        ep(d).wait_send()


def solve(part, damp):
    vmem = pl.BlockSpec(memory_space=VMEM)
    return pl.pallas_call(
        solve_kernel,
        out_shape=(
            jax.ShapeDtypeStruct((ROWS, COLS), F32),
            jax.ShapeDtypeStruct((ROWS, PICKED), F32),
        ),
        in_specs=[vmem] * 2,
        out_specs=(vmem, vmem),
        scratch_shapes=[
            VMEM((B, B), F32),
            VMEM((B, PICKED), F32),
            VMEM((B, PICKED), F32),
            VMEM((PICKED, PICKED), BF16),
            VMEM((PICKED, PICKED), BF16),
            VMEM((NG, B, B), BF16),
            VMEM((NG, B, B), BF16),
            VMEM((PICKED, SIDE), BF16),
            VMEM((PICKED, SIDE), BF16),
            VMEM((NY - 1, LEFT, RIGHT), F32),
            VMEM((NG, NZ, NY, PT, PG), F32),
            VMEM((NZ, NY, PT, GC), F32),
            VMEM((NG, COLS, PG), F32),
            VMEM((B, GC), F32),
        ]
        + [DMA((4, NY))] * 2
        + [DMA((NZ,))] * 2
        + [DMA((NZ, NY))] * 2
        + [DMA((NZ, NX))] * 4
        + [DMA((NZ,))] * 2
        + [DMA((NZ, NY))] * 2
        + [DMA((NX,))] * 4,
        compiler_params=pltpu.CompilerParams(
            collective_id=1, has_side_effects=True, vmem_limit_bytes=48 << 20
        ),
        name="solve",
    )(part, damp)


def shards(
    tx_fields, rx_fields, layer_of_cell, layer_cond, tx_of_row, rx_of_row, damping, panel_order
):
    g = lax.axis_index("grp")
    t = lax.axis_index("tile")
    z, y = t // NY, t % NY
    levels = jnp.arange(layer_cond.shape[0], dtype=jnp.int32)
    hit = levels[:, None] == layer_of_cell[None, :]
    cond = jnp.sum(jnp.where(hit, layer_cond[:, None], 0.0), axis=0, keepdims=True)
    fields = jnp.concatenate([tx_fields, rx_fields], axis=0).reshape(2, 96, CELLS)

    pair_of_row = tx_of_row * 128 + rx_of_row
    picks = jnp.concatenate(
        [
            lax.dynamic_slice_in_dim(panel_order, g * PG, PG),
            lax.dynamic_slice_in_dim(panel_order, z * (PT * NY), PT * NY),
        ]
    )
    chosen = picks[:, None] == jnp.arange(M, dtype=jnp.int32)[None, :]
    pair_picks = jnp.sum(jnp.where(chosen, pair_of_row[None, :], 0), axis=1)
    damp_picks = jnp.sum(jnp.where(chosen, damping[None, :], 0.0), axis=1)
    right = [
        pair_picks[:PG],
        lax.dynamic_slice_in_dim(pair_of_row, g * ROWS, ROWS),
        jnp.full((RIGHT - PG - ROWS,), -1, jnp.int32),
    ]
    near = lax.dynamic_slice_in_dim(pair_of_row, z * (COLS * NY), COLS * NY).reshape(NY, COLS)
    left = jnp.concatenate([near, pair_picks[PG:].reshape(NY, PT)], axis=1).reshape(-1)
    pairs = jnp.concatenate(right + [left])[:, None]
    tx_hot = (pairs // 128 == jnp.arange(64)[None, :]).astype(BF16)
    rx_hot = ((pairs % 128 == jnp.arange(128)[None, :]) & (pairs >= 0)).astype(BF16)

    left_ids = jnp.concatenate(
        [t * COLS + jnp.arange(COLS), lax.dynamic_slice_in_dim(picks, PG + y * PT, PT)]
    )
    right_ids = jnp.concatenate(
        [picks[:PG], g * ROWS + jnp.arange(ROWS), jnp.full((RIGHT - PG - ROWS,), -1)]
    )
    left_damp = jnp.concatenate(
        [
            lax.dynamic_slice_in_dim(damping, t * COLS, COLS),
            lax.dynamic_slice_in_dim(damp_picks, PG + y * PT, PT),
        ]
    )
    damp = jnp.where(left_ids[:, None] == right_ids[None, :], left_damp[:, None], 0.0)

    part = gram_sums(fields, cond, tx_hot, rx_hot)
    return solve(part.reshape(NY, LEFT, RIGHT), damp)


def solution(mesh):
    placed = (P(None, "tile"), P(None, "tile"), P("tile"), P(), P(), P(), P(), P())
    return jax.shard_map(
        shards,
        mesh=mesh,
        in_specs=placed,
        out_specs=(P("grp", "tile"), P("grp", None)),
        check_vma=False,
    )
```

```python
import functools

import jax
import jax.numpy as jnp
from jax import lax
from jax.experimental import pallas as pl
from jax.experimental.pallas import tpu as pltpu
from jax.sharding import PartitionSpec as P

F32 = jnp.float32
BF16 = jnp.bfloat16
MESH = pl.DeviceIdType.MESH
VMEM = pltpu.VMEM
DMA = pltpu.SemaphoreType.DMA

M = 2816
NCELLS = 32768
PICKED = 1024
NX, NY, NZ, NCORE = 4, 4, 8, 2
NG = NX * NCORE
NT = NY * NZ
ROWS = M // NG
COLS = M // NT
PG = PICKED // NG
PT = PICKED // NT
CELLS = NCELLS // NT
RIGHT = 512
LEFT = COLS + PT
B = 128
GC = RIGHT - PG


def dot(a, b, ca, cb):
    return lax.dot_general(a, b, (((ca,), (cb,)), ((), ())), preferred_element_type=F32)


def split(x):
    hi = x.astype(BF16)
    return hi, (x - hi.astype(F32)).astype(BF16)


def places():
    g = lax.axis_index("grp")
    t = lax.axis_index("tile")
    return g // NCORE, g % NCORE, t // NY, t % NY


def at_z(z, y):
    return {"tile": lax.rem(z + NZ, NZ) * NY + y}


def greet(peers):
    barrier = pltpu.get_barrier_semaphore()
    for peer in peers:
        pl.semaphore_signal(barrier, inc=1, device_id=peer, device_id_type=MESH)
    pl.semaphore_wait(barrier, len(peers))


def sends(src, dst, send, recv, peer):
    return pltpu.make_async_remote_copy(
        src_ref=src, dst_ref=dst, send_sem=send, recv_sem=recv, device_id=peer, device_id_type=MESH
    )


def owner_of(z, i):
    hops = (i + 1) // 2
    return lax.rem(z + NZ + jnp.where(i % 2 == 1, -hops, hops), NZ)


MSGS = 3
ROW_STEP = 32


def look_up(at, table):
    lanes = lax.broadcasted_iota(jnp.int32, (at.shape[0], table.shape[1]), 1)
    return jnp.sum(jnp.where(at == lanes, table, 0.0), axis=1, keepdims=True)


def prepare(order_ref, tx_row_ref, rx_row_ref, damp_row_ref, tx_hot, rx_hot, damp, g, z, y, t):
    order = order_ref[:, 0:PICKED].astype(F32)
    txs, rxs = tx_row_ref[...].astype(F32), rx_row_ref[...].astype(F32)

    def rows(i, carry):
        begin = pl.multiple_of(i * ROW_STEP, ROW_STEP)
        r = begin + lax.broadcasted_iota(jnp.int32, (ROW_STEP, 1), 0)
        s = r - RIGHT
        part = (s >= LEFT).astype(jnp.int32) + (s >= 2 * LEFT).astype(jnp.int32) + (s >= 3 * LEFT).astype(jnp.int32)
        q = s - part * LEFT
        right = s < 0
        is_pick = (right & (r < PG)) | ((s >= 0) & (q >= COLS))
        place = jnp.where(right, g * PG + r, (z * NY + part) * PT + q - COLS)
        plain = jnp.where(right, g * ROWS + r - PG, (z * NY + part) * COLS + q)
        plain = jnp.where(right & (r >= PG + ROWS), -1, plain)
        picked = look_up(jnp.where(is_pick, place, -1), order).astype(jnp.int32)
        ids = jnp.where(is_pick, picked, plain)
        lanes = lax.broadcasted_iota(jnp.int32, (ROW_STEP, M), 1)
        hit = ids == lanes
        none = jnp.where(ids < 0, -1.0, 0.0)
        txv = jnp.sum(jnp.where(hit, txs, 0.0), axis=1, keepdims=True) + none
        rxv = jnp.sum(jnp.where(hit, rxs, 0.0), axis=1, keepdims=True) + none
        here = pl.ds(begin, ROW_STEP)
        lane = lax.broadcasted_iota(jnp.int32, (ROW_STEP, 128), 1).astype(F32)
        tx_hot[here, :] = jnp.where(txv == lane, 1.0, 0.0).astype(BF16)
        rx_hot[here, :] = jnp.where(rxv == lane, 1.0, 0.0).astype(BF16)
        return carry

    lax.fori_loop(0, (RIGHT + NY * LEFT) // ROW_STEP, rows, 0)

    q = lax.broadcasted_iota(jnp.int32, (LEFT, 1), 0)
    picked = look_up(jnp.where(q >= COLS, t * PT + q - COLS, -1), order).astype(jnp.int32)
    left = jnp.where(q >= COLS, picked, t * COLS + q)
    near = look_up(left, damp_row_ref[...])
    natural = lax.broadcasted_iota(jnp.int32, (1, GC), 1)
    natural = jnp.where(natural < ROWS, g * ROWS + natural, -1)
    right = jnp.concatenate([order_ref[:, pl.ds(pl.multiple_of(g * PG, PG), PG)], natural], axis=1)
    damp[...] = jnp.where(left == right, near, 0.0)


def gram_part(
    tx_ref, rx_ref, layer_ref, cond_ref, prep, part, held, conds, sens, tx_hot, rx_hot,
    ring_send, ring_recv, cond_send, cond_recv, pair_send, pair_recv, local,
):
    x, c, z, y = places()
    up, down, pair = at_z(z + 1, y), at_z(z + NZ - 1, y), {"grp": x * NCORE + 1 - c}

    def own(m):
        if m == 0:
            return tx_ref.at[pl.ds(pl.multiple_of(c * 32, 32), 32), :]
        return rx_ref.at[pl.ds(pl.multiple_of(c * 64 + (m - 1) * 32, 32), 32), :]

    def way(i, m):
        return i % 2 == 1 if i < NZ - 1 else m == 0

    def ring(i, m):
        first = i < 3
        rising = way(i, m)
        prior = i - 2 if i < NZ - 1 or rising else i - 1
        o = z if first else owner_of(z, prior)
        src = own(m) if first else held.at[o, c, m]
        return sends(src, held.at[o, c, m], ring_send.at[i, m], ring_recv.at[i, m], up if rising else down)

    def line(i):
        o = z if i < 3 else owner_of(z, i - 2)
        return sends(conds.at[o], conds.at[o], cond_send.at[i], cond_recv.at[i], up if i % 2 == 1 else down)

    def to_pair(i, m):
        o = owner_of(z, i)
        return sends(held.at[o, c, m], held.at[o, c, m], pair_send.at[i, m], pair_recv.at[i, m], pair)

    def arrive(i, m):
        ring(i, m).wait_recv()
        if i < NZ - 3:
            ring(i + 2, m).start()
        elif i < NZ - 1 and way(NZ - 1, m) == (i % 2 == 1):
            ring(NZ - 1, m).start()
        to_pair(i, m).start()
        if m == 0:
            line(i).wait_recv()
            if i + 2 < NZ:
                line(i + 2).start()

    for m in range(MSGS):
        ring(1, m).start()
        ring(2, m).start()
    mine = []
    for core in range(NCORE):
        mine.append(pltpu.make_async_copy(tx_ref.at[32 * core : 32 * core + 32, :], held.at[z, core, 0], local.at[core, 0]))
        for m in (1, 2):
            at = 64 * core + 32 * (m - 1)
            mine.append(pltpu.make_async_copy(rx_ref.at[at : at + 32, :], held.at[z, core, m], local.at[core, m]))
    for copy in mine:
        copy.start()
    layer = layer_ref[...]
    cond = jnp.zeros((1, CELLS), F32)
    for level in range(32):
        cond = jnp.where(layer == level, cond_ref[level], cond)
    conds[z] = cond
    line(1).start()
    line(2).start()
    prep()
    part[...] = jnp.zeros_like(part)
    for copy in mine:
        copy.wait()
    for m in range(MSGS):
        arrive(1, m)

    def body(i, carry):
        for n in range(NZ - 1):
            @pl.when(i == n)
            def _():
                for m in range(MSGS):
                    if n + 2 < NZ - 1:
                        arrive(n + 2, m)
                    elif way(NZ - 1, m) == (n % 2 == 1):
                        arrive(NZ - 1, m)

        for n in range(1, NZ):
            @pl.when(i == n)
            def _():
                for m in range(MSGS):
                    to_pair(n, m).wait_recv()

        o = owner_of(z, i)
        width = 256

        def chunk(j, carry):
            at = pl.ds(pl.multiple_of(j * width, width), width)
            txs = jnp.concatenate([held[o, k, 0, :, at] for k in range(NCORE)], axis=0)
            rxs = jnp.concatenate([held[o, k, m, :, at] for k in range(NCORE) for m in (1, 2)], axis=0)
            both = dot(tx_hot[:, 0:64], txs, 1, 0) * dot(rx_hot[...], rxs, 1, 0)
            sens[:, at] = (both * conds[o, :, at]).astype(BF16)
            return carry

        lax.fori_loop(0, CELLS // width, chunk, 0)
        part[...] += dot(sens[RIGHT:, :], sens[0:RIGHT, :], 1, 1).reshape(NY, LEFT, RIGHT)
        return carry

    lax.fori_loop(0, NZ, body, 0)

    def finish():
        for i in range(1, NZ):
            for m in range(MSGS):
                ring(i, m).wait_send()
                to_pair(i, m).wait_send()
            line(i).wait_send()

    return finish


def tree(vs):
    while len(vs) > 1:
        vs = [vs[i] + vs[i + 1] if i + 1 < len(vs) else vs[i] for i in range(0, len(vs), 2)]
    return vs[0]


def inverse_factor(m):
    W = 16
    H = W // 8
    lane = lax.broadcasted_iota(jnp.int32, (8, B), 1)
    sub = lax.broadcasted_iota(jnp.int32, (8, B), 0)
    tiles = [m[8 * i : 8 * i + 8, :] for i in range(B // 8)]
    full = lambda v: jnp.broadcast_to(v, (8, B))
    column = lambda t, j: jnp.take_along_axis(t, jnp.full((8, B), j, jnp.int32), axis=1)
    for j in range(0, B, W):
        q = j // 8
        here = (lane >= j) & (lane < j + W)
        cs = {}
        for p in range(W):
            for h in range(p // 8, H):
                cs[p, h] = column(tiles[q + h], j + p)
        rows = [
            jnp.where(lane == j + 8 * h + sub, 1.0, jnp.where(here, 0.0, tiles[q + h])) for h in range(H)
        ]
        pivots, inverses, solved, low = [], [], [], {}
        for p in range(W):
            hp, s = divmod(p, 8)
            pivot = full(cs[p, hp][s : s + 1, :])
            inverse = 1.0 / pivot
            pivots.append(pivot)
            inverses.append(inverse)
            row = full(rows[hp][s : s + 1, :])
            solved.append(row)
            for k in range(p + 1, W):
                low[k, p] = full(cs[p, k // 8][k % 8 : k % 8 + 1, :]) * inverse
                for h in range(k // 8, H):
                    cs[k, h] = cs[k, h] - cs[p, h] * low[k, p]
            scaled = row * inverse
            for h in range(hp, H):
                if h == hp and s == 7:
                    continue
                f = jnp.where(sub > s, cs[p, h], 0.0) if h == hp else cs[p, h]
                rows[h] = rows[h] - f * scaled
        back = [None] * W
        for p in reversed(range(W)):
            v = solved[p] * inverses[p]
            for i in reversed(range(p + 1, W)):
                v = v - low[i, p] * back[i]
            back[p] = v
        for i in range(q + H, B // 8):
            terms = [column(tiles[i], j + p) * back[p] for p in range(W)]
            tiles[i] = jnp.where(here, 0.0, tiles[i]) - tree(terms)
        for h in range(H):
            scale = pivots[8 * h]
            for s in range(1, 8):
                scale = jnp.where(sub == s, pivots[8 * h + s], scale)
            tiles[q + h] = rows[h] * lax.rsqrt(scale)
    w = jnp.concatenate(tiles, axis=0)
    r = lax.broadcasted_iota(jnp.int32, (B, B), 0)
    c = lax.broadcasted_iota(jnp.int32, (B, B), 1)
    return jnp.where(r >= c, w, 0.0)


SIDE = GC + B


def dot3(ah, al, bh, bl, ca, cb):
    return dot(ah, bh, ca, cb) + (dot(ah, bl, ca, cb) + dot(al, bh, ca, cb))


def block_of(k):
    return pl.ds(pl.multiple_of(k * B, B), B)


DIAG, PICK, CROSS, REST = 0, 1, 2, 3
PARTS = (
    (slice(COLS, LEFT), slice(0, PG)),
    (slice(COLS, LEFT), slice(PG, RIGHT)),
    (slice(0, COLS), slice(0, PG)),
    (slice(0, COLS), slice(PG, RIGHT)),
)


def step_kernel(
    tx_ref, rx_ref, layer_ref, cond_ref, tx_row_ref, rx_row_ref, damp_row_ref, order_ref,
    trail_ref, factor_ref,
    part_ref, damp_ref, held, conds, sens, tx_hot, rx_hot,
    gr_send, gr_recv, gc_send, gc_recv, gp_send, gp_recv, local,
    now, acc, nxt, high, low, wh, wl, xh, xl, got, diag, side_rows, cross, rest,
    rs_send, rs_recv, dz_send, dz_recv, dy_send, dy_recv, dx_send, dx_recv, dp_send, dp_recv,
    cz_send, cz_recv, cy_send, cy_recv, ex_send, ex_recv, ep_send, ep_recv,
):
    x, c, z, y = places()
    g = x * NCORE + c
    pair = {"grp": x * NCORE + 1 - c}
    at_y = [None] + [{"tile": z * NY + lax.rem(y + d, NY)} for d in range(1, NY)]
    at_x = [None] + [{"grp": lax.rem(x + d, NX) * NCORE + c} for d in range(1, NX)]
    in_z = [None] + [{"tile": lax.rem(z + d, NZ) * NY + y} for d in range(1, NZ)]
    greet(at_y[1:] + at_x[1:] + in_z[1:] + [pair])

    def prep():
        prepare(
            order_ref, tx_row_ref, rx_row_ref, damp_row_ref, tx_hot, rx_hot, damp_ref, g, z, y, z * NY + y
        )

    finish = gram_part(
        tx_ref, rx_ref, layer_ref, cond_ref, prep, part_ref, held, conds, sens, tx_hot, rx_hot,
        gr_send, gr_recv, gc_send, gc_recv, gp_send, gp_recv, local,
    )

    def rs(p, d):
        rows, cols = PARTS[p]
        return sends(
            part_ref.at[lax.rem(y + d, NY), rows, cols], got.at[d - 1, rows, cols],
            rs_send.at[p, d], rs_recv.at[p, d], at_y[d],
        )

    def start_sums(p):
        for d in range(1, NY):
            rs(p, d).start()

    def summed(p):
        rows, cols = PARTS[p]
        total = part_ref[y, rows, cols]
        for d in range(1, NY):
            rs(p, d).wait_recv()
            total += got[d - 1, rows, cols]
        return total * (1.0 / NCELLS) + damp_ref[rows, cols]

    def dz(d):
        return sends(diag.at[g, z, y], diag.at[g, z, y], dz_send.at[d], dz_recv.at[d], in_z[d])

    def dy(zz, d):
        return sends(diag.at[g, zz, y], diag.at[g, zz, y], dy_send.at[zz, d], dy_recv.at[zz, d], at_y[d])

    def dx(zz, d):
        return sends(diag.at[g, zz], diag.at[g, zz], dx_send.at[zz, d], dx_recv.at[zz, d], at_x[d])

    def dp(zz, d):
        gd = lax.rem(x + NX - d, NX) * NCORE + c
        return sends(diag.at[gd, zz], diag.at[gd, zz], dp_send.at[zz, d], dp_recv.at[zz, d], pair)

    def cz(d):
        return sends(side_rows.at[z, y], side_rows.at[z, y], cz_send.at[d], cz_recv.at[d], in_z[d])

    def cy(zz, d):
        return sends(side_rows.at[zz, y], side_rows.at[zz, y], cy_send.at[zz, d], cy_recv.at[zz, d], at_y[d])

    def ex(d):
        return sends(cross.at[g], cross.at[g], ex_send.at[d], ex_recv.at[d], at_x[d])

    def ep(d):
        gd = lax.rem(x + NX - d, NX) * NCORE + c
        return sends(cross.at[gd], cross.at[gd], ep_send.at[d], ep_recv.at[d], pair)

    def arrived(zz, copy, sem_recv, ref):
        d = lax.rem(z + NZ - zz, NZ)

        @pl.when(d != 0)
        def _():
            sends(ref.at[zz, y], ref.at[zz, y], sem_recv.at[d], sem_recv.at[d], pair).wait_recv()

    def across(zz):
        for d in range(1, NX):
            dx(zz, d).wait_recv()
            dp(zz, d).start()

    def complete(zz):
        for d in range(NX):
            dp(zz, d).wait_recv()

    start_sums(DIAG)
    high[...] = jnp.zeros_like(high)
    low[...] = jnp.zeros_like(low)
    xh[...] = jnp.zeros_like(xh)
    xl[...] = jnp.zeros_like(xl)
    acc[...] = jnp.zeros_like(acc)
    wh[0] = jnp.zeros((B, B), BF16)
    wl[0] = jnp.zeros((B, B), BF16)
    diag[g, z, y] = summed(DIAG)
    for d in range(1, NZ):
        dz(d).start()
    start_sums(PICK)
    for zz in range(NZ):
        arrived(zz, None, dz_recv, diag.at[g])
        for d in range(1, NY):
            dy(zz, d).start()
    start_sums(CROSS)
    for zz in range(NZ):
        for d in range(1, NY):
            dy(zz, d).wait_recv()
        for d in range(1, NX):
            dx(zz, d).start()
        dp(zz, 0).start()
    start_sums(REST)
    across(0)
    across(1)
    complete(0)

    def diag_rows(k, begin):
        return jnp.concatenate([diag[i, k].reshape(B, B) for i in range(begin, NG)], axis=1)

    nxt[...] = diag_rows(0, 0)
    now[...] = diag[0, 0].reshape(B, B)

    def block(k, begin, depth):
        w = inverse_factor(now[...])
        last = jnp.maximum(k - 1, 0)
        cols = slice(begin * B, PICKED)
        ah, al = split(acc[:, cols])
        uh, ul = split(dot3(wh[last], wl[last], ah, al, 1, 0))
        high[block_of(last), cols] = uh
        low[block_of(last), cols] = ul
        at = block_of(k)
        acc[:, cols] = nxt[:, cols] - dot3(high[block_of(last), at], low[block_of(last), at], uh, ul, 0, 0)
        after = jnp.minimum(k + 1, NG - 1)
        there = block_of(after)
        nxt[:, cols] = diag_rows(after, begin) - dot3(
            high[0:depth, there], low[0:depth, there], high[0:depth, cols], low[0:depth, cols], 0, 0
        )
        nh, nl = split(w)
        wh[k] = nh
        wl[k] = nl
        bh, bl = split(acc[:, there])
        vh, vl = split(dot3(nh, nl, bh, bl, 1, 0))
        now[...] = nxt[:, there] - dot3(vh, vl, vh, vl, 0, 0)

    def side(i, depth):
        at = block_of(i)
        padded = jnp.concatenate([cross[i], jnp.zeros((B - COLS, B), F32)], axis=0).T
        start = jnp.concatenate([side_rows[i].reshape(B, GC), padded], axis=1)
        done = dot3(high[0:depth, at], low[0:depth, at], xh[0:depth, :], xl[0:depth, :], 0, 0)
        sh, sl = split(start - done)
        u = dot3(wh[i], wl[i], sh, sl, 1, 0)
        uh, ul = split(u)
        xh[at, :] = uh
        xl[at, :] = ul
        factor_ref[:, at] = u[:, 0:GC].T[0:ROWS, :]

    def first(k, carry):
        across(k + 2)
        complete(k + 1)

        @pl.when(k == 0)
        def _():
            side_rows[z, y] = summed(PICK)
            for d in range(1, NZ):
                cz(d).start()
            cross[g] = summed(CROSS)
            for d in range(1, NX):
                ex(d).start()
            ep(0).start()

        @pl.when(k == 2)
        def _():
            for zz in range(NZ):
                arrived(zz, None, cz_recv, side_rows)
                for d in range(1, NY):
                    cy(zz, d).start()
            for d in range(1, NX):
                ex(d).wait_recv()
                ep(d).start()

        block(k, 0, 4 * B)
        return carry

    def here(i):
        for d in range(1, NY):
            cy(i, d).wait_recv()

    def second(k, carry):
        across(k + 2)
        complete(k + 1)
        i = 2 * (k - 4)
        here(i)
        here(i + 1)
        block(k, 3, 5 * B)
        side(i, 4 * B)
        side(i + 1, 4 * B)
        return carry

    def third(k, carry):
        @pl.when(k < NG - 1)
        def _():
            complete(k + 1)

        here(k - 2)
        block(k, 5, 7 * B)
        side(k - 2, 6 * B)
        return carry

    lax.fori_loop(0, 4, first, 0)
    for d in range(NX):
        ep(d).wait_recv()
    lax.fori_loop(4, 6, second, 0)
    lax.fori_loop(6, NG, third, 0)
    here(NG - 2)
    here(NG - 1)
    side(NG - 2, 6 * B)
    side(NG - 1, 7 * B)
    rest[0:COLS, :] = summed(REST)
    rest[COLS:, :] = jnp.zeros((B - COLS, GC), F32)
    drop = dot3(xh[:, 0:GC], xl[:, 0:GC], xh[:, GC:], xl[:, GC:], 0, 0)
    trail_ref[...] = (rest[...].T - drop)[0:ROWS, 0:COLS]

    finish()
    for d in range(1, NY):
        for p in range(4):
            rs(p, d).wait_send()
        for zz in range(NZ):
            dy(zz, d).wait_send()
            cy(zz, d).wait_send()
    for d in range(1, NZ):
        dz(d).wait_send()
        cz(d).wait_send()
    for d in range(NX):
        for zz in range(NZ):
            if d:
                dx(zz, d).wait_send()
            dp(zz, d).wait_send()
        if d:
            ex(d).wait_send()
        ep(d).wait_send()


def shards(
    tx_fields, rx_fields, layer_of_cell, layer_cond, tx_of_row, rx_of_row, damping, panel_order
):
    vmem = pl.BlockSpec(memory_space=VMEM)
    smem = pl.BlockSpec(memory_space=pltpu.SMEM)
    return pl.pallas_call(
        step_kernel,
        out_shape=(
            jax.ShapeDtypeStruct((ROWS, COLS), F32),
            jax.ShapeDtypeStruct((ROWS, PICKED), F32),
        ),
        in_specs=[vmem, vmem, vmem, smem, vmem, vmem, vmem, vmem],
        out_specs=(vmem, vmem),
        scratch_shapes=[
            VMEM((NY, LEFT, RIGHT), F32),
            VMEM((LEFT, RIGHT), F32),
            VMEM((NZ, NCORE, MSGS, 32, CELLS), BF16),
            VMEM((NZ, 1, CELLS), F32),
            VMEM((RIGHT + NY * LEFT, CELLS), BF16),
            VMEM((RIGHT + NY * LEFT, 128), BF16),
            VMEM((RIGHT + NY * LEFT, 128), BF16),
        ]
        + [DMA((NZ, MSGS))] * 2
        + [DMA((NZ,))] * 2
        + [DMA((NZ, MSGS))] * 2
        + [DMA((NCORE, MSGS))]
        + [
            VMEM((B, B), F32),
            VMEM((B, PICKED), F32),
            VMEM((B, PICKED), F32),
            VMEM((PICKED, PICKED), BF16),
            VMEM((PICKED, PICKED), BF16),
            VMEM((NG, B, B), BF16),
            VMEM((NG, B, B), BF16),
            VMEM((PICKED, SIDE), BF16),
            VMEM((PICKED, SIDE), BF16),
            VMEM((NY - 1, LEFT, RIGHT), F32),
            VMEM((NG, NZ, NY, PT, PG), F32),
            VMEM((NZ, NY, PT, GC), F32),
            VMEM((NG, COLS, PG), F32),
            VMEM((B, GC), F32),
        ]
        + [DMA((4, NY))] * 2
        + [DMA((NZ,))] * 2
        + [DMA((NZ, NY))] * 2
        + [DMA((NZ, NX))] * 4
        + [DMA((NZ,))] * 2
        + [DMA((NZ, NY))] * 2
        + [DMA((NX,))] * 4,
        compiler_params=pltpu.CompilerParams(
            collective_id=0, has_side_effects=True, vmem_limit_bytes=56 << 20
        ),
        name="step",
    )(
        tx_fields, rx_fields, layer_of_cell[None, :], layer_cond,
        tx_of_row[None, :], rx_of_row[None, :], damping[None, :], panel_order[None, :],
    )


def solution(mesh):
    placed = (P(None, "tile"), P(None, "tile"), P("tile"), P(), P(), P(), P(), P())
    return jax.shard_map(
        shards,
        mesh=mesh,
        in_specs=placed,
        out_specs=(P("grp", "tile"), P("grp", None)),
        check_vma=False,
    )
```

```python
import functools

import jax
import jax.numpy as jnp
from jax import lax
from jax.experimental import pallas as pl
from jax.experimental.pallas import tpu as pltpu
from jax.sharding import PartitionSpec as P

F32 = jnp.float32
BF16 = jnp.bfloat16
MESH = pl.DeviceIdType.MESH
VMEM = pltpu.VMEM
DMA = pltpu.SemaphoreType.DMA

M = 2816
NCELLS = 32768
PICKED = 1024
NX, NY, NZ, NCORE = 4, 4, 8, 2
NG = NX * NCORE
NT = NY * NZ
ROWS = M // NG
COLS = M // NT
PG = PICKED // NG
PT = PICKED // NT
CELLS = NCELLS // NT
RIGHT = 512
LEFT = COLS + PT
B = 128
GC = RIGHT - PG


def dot(a, b, ca, cb):
    return lax.dot_general(a, b, (((ca,), (cb,)), ((), ())), preferred_element_type=F32)


def split(x):
    hi = x.astype(BF16)
    return hi, (x - hi.astype(F32)).astype(BF16)


def places():
    g = lax.axis_index("grp")
    t = lax.axis_index("tile")
    return g // NCORE, g % NCORE, t // NY, t % NY


def at_z(z, y):
    return {"tile": lax.rem(z + NZ, NZ) * NY + y}


def greet(peers):
    barrier = pltpu.get_barrier_semaphore()
    for peer in peers:
        pl.semaphore_signal(barrier, inc=1, device_id=peer, device_id_type=MESH)
    pl.semaphore_wait(barrier, len(peers))


def sends(src, dst, send, recv, peer):
    return pltpu.make_async_remote_copy(
        src_ref=src, dst_ref=dst, send_sem=send, recv_sem=recv, device_id=peer, device_id_type=MESH
    )


def owner_of(z, i):
    hops = (i + 1) // 2
    return lax.rem(z + NZ + jnp.where(i % 2 == 1, -hops, hops), NZ)


MSGS = 3
LINES = 24


def look_up(ids, tables):
    count = ids.shape[0]
    lanes = lax.broadcasted_iota(jnp.int32, (count, 128), 1)
    line = jnp.where((ids >> 7) == lanes, 1.0, 0.0).astype(BF16)[:, 0:LINES]
    found = dot(line, jnp.concatenate(tables, axis=1).astype(BF16), 1, 0)
    mine = (ids & 127) == lanes
    return [
        jnp.sum(jnp.where(mine, found[:, 128 * i : 128 * i + 128], 0.0), axis=1, keepdims=True)
        for i in range(len(tables))
    ]


def column(row):
    at = [lax.broadcasted_iota(jnp.int32, (128, 128), d) for d in (0, 1)]
    return jnp.sum(jnp.where(at[0] == at[1], row, 0.0), axis=1, keepdims=True)


def prepare(tx_list, rx_list, damp_list, order, tx_hot, rx_hot, damp, g, z, y, t):
    def run(begin, count):
        return begin + lax.broadcasted_iota(jnp.int32, (count, 1), 0)

    right_row = order[pl.ds(g, 1), :].astype(F32)
    left_picks = column(order[pl.ds(z, 1), :].astype(F32)).astype(jnp.int32)
    ids = [column(right_row).astype(jnp.int32), run(g * ROWS, ROWS), run(0, RIGHT - PG - ROWS) * 0 - 1]
    for j in range(NY):
        ids += [run((z * NY + j) * COLS, COLS), left_picks[PT * j : PT * j + PT, :]]
    ids = jnp.concatenate(ids, axis=0)
    txv, rxv = look_up(ids, [v[...].astype(F32) for v in (tx_list, rx_list)])
    none = jnp.where(ids < 0, -1.0, 0.0)
    lane = lax.broadcasted_iota(jnp.int32, (RIGHT + NY * LEFT, 128), 1).astype(F32)
    tx_hot[...] = jnp.where(txv + none == lane, 1.0, 0.0).astype(BF16)
    rx_hot[...] = jnp.where(rxv + none == lane, 1.0, 0.0).astype(BF16)

    own_picks = sum(jnp.where(y == j, left_picks[PT * j : PT * j + PT, :], 0) for j in range(NY))
    left = jnp.concatenate([run(t * COLS, COLS), own_picks], axis=0)
    table = damp_list[...]
    high = table.astype(BF16).astype(F32)
    mid = (table - high).astype(BF16).astype(F32)
    terms = look_up(left, [high, mid, table - high - mid])
    near = terms[0] + (terms[1] + terms[2])
    natural = lax.broadcasted_iota(jnp.int32, (1, GC), 1)
    natural = jnp.where(natural < ROWS, g * ROWS + natural, -1)
    right = jnp.concatenate([right_row.astype(jnp.int32), natural], axis=1)
    damp[...] = jnp.where(left == right, near, 0.0)


def gram_part(
    tx_ref, rx_ref, layer_ref, cond_ref, prep, part, held, conds, sens, tx_hot, rx_hot,
    ring_send, ring_recv, cond_send, cond_recv, pair_send, pair_recv, local,
):
    x, c, z, y = places()
    up, down, pair = at_z(z + 1, y), at_z(z + NZ - 1, y), {"grp": x * NCORE + 1 - c}

    def own(m):
        if m == 0:
            return tx_ref.at[pl.ds(pl.multiple_of(c * 32, 32), 32), :]
        return rx_ref.at[pl.ds(pl.multiple_of(c * 64 + (m - 1) * 32, 32), 32), :]

    def way(i, m):
        return i % 2 == 1 if i < NZ - 1 else m == 0

    def ring(i, m):
        first = i < 3
        rising = way(i, m)
        prior = i - 2 if i < NZ - 1 or rising else i - 1
        o = z if first else owner_of(z, prior)
        src = own(m) if first else held.at[o, c, m]
        return sends(src, held.at[o, c, m], ring_send.at[i, m], ring_recv.at[i, m], up if rising else down)

    def line(i):
        o = z if i < 3 else owner_of(z, i - 2)
        return sends(conds.at[o], conds.at[o], cond_send.at[i], cond_recv.at[i], up if i % 2 == 1 else down)

    def to_pair(i, m):
        o = owner_of(z, i)
        return sends(held.at[o, c, m], held.at[o, c, m], pair_send.at[i, m], pair_recv.at[i, m], pair)

    def arrive(i, m):
        ring(i, m).wait_recv()
        if i < NZ - 3:
            ring(i + 2, m).start()
        elif i < NZ - 1 and way(NZ - 1, m) == (i % 2 == 1):
            ring(NZ - 1, m).start()
        to_pair(i, m).start()
        if m == 0:
            line(i).wait_recv()
            if i + 2 < NZ:
                line(i + 2).start()

    for m in range(MSGS):
        ring(1, m).start()
        ring(2, m).start()
    mine = []
    for core in range(NCORE):
        mine.append(pltpu.make_async_copy(tx_ref.at[32 * core : 32 * core + 32, :], held.at[z, core, 0], local.at[core, 0]))
        for m in (1, 2):
            at = 64 * core + 32 * (m - 1)
            mine.append(pltpu.make_async_copy(rx_ref.at[at : at + 32, :], held.at[z, core, m], local.at[core, m]))
    for copy in mine:
        copy.start()
    layer = layer_ref[...]
    cond = jnp.zeros(layer.shape, F32)
    for level in range(32):
        cond = jnp.where(layer == level, cond_ref[level], cond)
    conds[z] = jnp.concatenate([cond[r : r + 1, :] for r in range(CELLS // 128)], axis=1)
    line(1).start()
    line(2).start()
    prep()
    part[...] = jnp.zeros_like(part)
    for copy in mine:
        copy.wait()
    for m in range(MSGS):
        arrive(1, m)

    def body(i, carry):
        for n in range(NZ - 1):
            @pl.when(i == n)
            def _():
                for m in range(MSGS):
                    if n + 2 < NZ - 1:
                        arrive(n + 2, m)
                    elif way(NZ - 1, m) == (n % 2 == 1):
                        arrive(NZ - 1, m)

        for n in range(1, NZ):
            @pl.when(i == n)
            def _():
                for m in range(MSGS):
                    to_pair(n, m).wait_recv()

        o = owner_of(z, i)
        txs = jnp.concatenate([held[o, k, 0] for k in range(NCORE)], axis=0)
        rxs = jnp.concatenate([held[o, k, m] for k in range(NCORE) for m in (1, 2)], axis=0)
        both = dot(tx_hot[:, 0:64], txs, 1, 0) * dot(rx_hot[...], rxs, 1, 0)
        sens[...] = (both * conds[o]).astype(BF16)
        part[...] += dot(sens[RIGHT:, :], sens[0:RIGHT, :], 1, 1).reshape(NY, LEFT, RIGHT)
        return carry

    lax.fori_loop(0, NZ, body, 0)

    def finish():
        for i in range(1, NZ):
            for m in range(MSGS):
                ring(i, m).wait_send()
                to_pair(i, m).wait_send()
            line(i).wait_send()

    return finish


def tree(vs):
    while len(vs) > 1:
        vs = [vs[i] + vs[i + 1] if i + 1 < len(vs) else vs[i] for i in range(0, len(vs), 2)]
    return vs[0]


def inverse_factor(m):
    W = 16
    H = W // 8
    lane = lax.broadcasted_iota(jnp.int32, (8, B), 1)
    sub = lax.broadcasted_iota(jnp.int32, (8, B), 0)
    tiles = [m[8 * i : 8 * i + 8, :] for i in range(B // 8)]
    full = lambda v: jnp.broadcast_to(v, (8, B))
    column = lambda t, j: jnp.take_along_axis(t, jnp.full((8, B), j, jnp.int32), axis=1)
    for j in range(0, B, W):
        q = j // 8
        here = (lane >= j) & (lane < j + W)
        cs = {}
        for p in range(W):
            for h in range(p // 8, H):
                cs[p, h] = column(tiles[q + h], j + p)
        rows = [
            jnp.where(lane == j + 8 * h + sub, 1.0, jnp.where(here, 0.0, tiles[q + h])) for h in range(H)
        ]
        pivots, inverses, solved, low = [], [], [], {}
        for p in range(W):
            hp, s = divmod(p, 8)
            pivot = full(cs[p, hp][s : s + 1, :])
            inverse = 1.0 / pivot
            pivots.append(pivot)
            inverses.append(inverse)
            row = full(rows[hp][s : s + 1, :])
            solved.append(row)
            for k in range(p + 1, W):
                low[k, p] = full(cs[p, k // 8][k % 8 : k % 8 + 1, :]) * inverse
                for h in range(k // 8, H):
                    cs[k, h] = cs[k, h] - cs[p, h] * low[k, p]
            scaled = row * inverse
            for h in range(hp, H):
                if h == hp and s == 7:
                    continue
                f = jnp.where(sub > s, cs[p, h], 0.0) if h == hp else cs[p, h]
                rows[h] = rows[h] - f * scaled
        back = [None] * W
        for p in reversed(range(W)):
            v = solved[p] * inverses[p]
            for i in reversed(range(p + 1, W)):
                v = v - low[i, p] * back[i]
            back[p] = v
        for i in range(q + H, B // 8):
            terms = [column(tiles[i], j + p) * back[p] for p in range(W)]
            tiles[i] = jnp.where(here, 0.0, tiles[i]) - tree(terms)
        for h in range(H):
            scale = pivots[8 * h]
            for s in range(1, 8):
                scale = jnp.where(sub == s, pivots[8 * h + s], scale)
            tiles[q + h] = rows[h] * lax.rsqrt(scale)
    w = jnp.concatenate(tiles, axis=0)
    r = lax.broadcasted_iota(jnp.int32, (B, B), 0)
    c = lax.broadcasted_iota(jnp.int32, (B, B), 1)
    return jnp.where(r >= c, w, 0.0)


SIDE = GC + B


def dot3(ah, al, bh, bl, ca, cb):
    return dot(ah, bh, ca, cb) + (dot(ah, bl, ca, cb) + dot(al, bh, ca, cb))


def block_of(k):
    return pl.ds(pl.multiple_of(k * B, B), B)


DIAG, PICK, CROSS, REST = 0, 1, 2, 3
PARTS = (
    (slice(COLS, LEFT), slice(0, PG)),
    (slice(COLS, LEFT), slice(PG, RIGHT)),
    (slice(0, COLS), slice(0, PG)),
    (slice(0, COLS), slice(PG, RIGHT)),
)


def step_kernel(
    tx_ref, rx_ref, layer_ref, cond_ref, tx_list, rx_list, damp_list, order,
    trail_ref, factor_ref,
    part_ref, damp_ref, held, conds, sens, tx_hot, rx_hot,
    gr_send, gr_recv, gc_send, gc_recv, gp_send, gp_recv, local,
    now, acc, nxt, high, low, wh, wl, xh, xl, got, diag, side_rows, cross,
    rs_send, rs_recv, dz_send, dz_recv, dy_send, dy_recv, dx_send, dx_recv, dp_send, dp_recv,
    cz_send, cz_recv, cy_send, cy_recv, ex_send, ex_recv, ep_send, ep_recv,
):
    x, c, z, y = places()
    g = x * NCORE + c
    pair = {"grp": x * NCORE + 1 - c}
    at_y = [None] + [{"tile": z * NY + lax.rem(y + d, NY)} for d in range(1, NY)]
    at_x = [None] + [{"grp": lax.rem(x + d, NX) * NCORE + c} for d in range(1, NX)]
    in_z = [None] + [{"tile": lax.rem(z + d, NZ) * NY + y} for d in range(1, NZ)]
    greet(at_y[1:] + at_x[1:] + in_z[1:] + [pair])

    def prep():
        prepare(tx_list, rx_list, damp_list, order, tx_hot, rx_hot, damp_ref, g, z, y, z * NY + y)

    finish = gram_part(
        tx_ref, rx_ref, layer_ref, cond_ref, prep, part_ref, held, conds, sens, tx_hot, rx_hot,
        gr_send, gr_recv, gc_send, gc_recv, gp_send, gp_recv, local,
    )

    def rs(p, d):
        rows, cols = PARTS[p]
        return sends(
            part_ref.at[lax.rem(y + d, NY), rows, cols], got.at[d - 1, rows, cols],
            rs_send.at[p, d], rs_recv.at[p, d], at_y[d],
        )

    def start_sums(p):
        for d in range(1, NY):
            rs(p, d).start()

    def summed(p):
        rows, cols = PARTS[p]
        total = part_ref[y, rows, cols]
        for d in range(1, NY):
            rs(p, d).wait_recv()
            total += got[d - 1, rows, cols]
        return total * (1.0 / NCELLS) + damp_ref[rows, cols]

    def dz(d):
        return sends(diag.at[g, z, y], diag.at[g, z, y], dz_send.at[d], dz_recv.at[d], in_z[d])

    def dy(zz, d):
        return sends(diag.at[g, zz, y], diag.at[g, zz, y], dy_send.at[zz, d], dy_recv.at[zz, d], at_y[d])

    def dx(zz, d):
        return sends(diag.at[g, zz], diag.at[g, zz], dx_send.at[zz, d], dx_recv.at[zz, d], at_x[d])

    def dp(zz, d):
        gd = lax.rem(x + NX - d, NX) * NCORE + c
        return sends(diag.at[gd, zz], diag.at[gd, zz], dp_send.at[zz, d], dp_recv.at[zz, d], pair)

    def cz(d):
        return sends(side_rows.at[z, y], side_rows.at[z, y], cz_send.at[d], cz_recv.at[d], in_z[d])

    def cy(zz, d):
        return sends(side_rows.at[zz, y], side_rows.at[zz, y], cy_send.at[zz, d], cy_recv.at[zz, d], at_y[d])

    def ex(d):
        return sends(cross.at[g], cross.at[g], ex_send.at[d], ex_recv.at[d], at_x[d])

    def ep(d):
        gd = lax.rem(x + NX - d, NX) * NCORE + c
        return sends(cross.at[gd], cross.at[gd], ep_send.at[d], ep_recv.at[d], pair)

    def arrived(zz, copy, sem_recv, ref):
        d = lax.rem(z + NZ - zz, NZ)

        @pl.when(d != 0)
        def _():
            sends(ref.at[zz, y], ref.at[zz, y], sem_recv.at[d], sem_recv.at[d], pair).wait_recv()

    def across(zz):
        for d in range(1, NX):
            dx(zz, d).wait_recv()
            dp(zz, d).start()

    def complete(zz):
        for d in range(NX):
            dp(zz, d).wait_recv()

    start_sums(DIAG)
    high[...] = jnp.zeros_like(high)
    low[...] = jnp.zeros_like(low)
    xh[...] = jnp.zeros_like(xh)
    xl[...] = jnp.zeros_like(xl)
    acc[...] = jnp.zeros_like(acc)
    wh[0] = jnp.zeros((B, B), BF16)
    wl[0] = jnp.zeros((B, B), BF16)
    diag[g, z, y] = summed(DIAG)
    for d in range(1, NZ):
        dz(d).start()
    start_sums(PICK)
    for zz in range(NZ):
        arrived(zz, None, dz_recv, diag.at[g])
        for d in range(1, NY):
            dy(zz, d).start()
    start_sums(CROSS)
    for zz in range(NZ):
        for d in range(1, NY):
            dy(zz, d).wait_recv()
        for d in range(1, NX):
            dx(zz, d).start()
        dp(zz, 0).start()
    start_sums(REST)
    across(0)
    across(1)
    complete(0)

    def diag_rows(k, begin):
        return jnp.concatenate([diag[i, k].reshape(B, B) for i in range(begin, NG)], axis=1)

    nxt[...] = diag_rows(0, 0)
    now[...] = diag[0, 0].reshape(B, B)

    def block(k, begin, depth):
        w = inverse_factor(now[...])
        last = jnp.maximum(k - 1, 0)
        cols = slice(begin * B, PICKED)
        ah, al = split(acc[:, cols])
        uh, ul = split(dot3(wh[last], wl[last], ah, al, 1, 0))
        high[block_of(last), cols] = uh
        low[block_of(last), cols] = ul
        at = block_of(k)
        acc[:, cols] = nxt[:, cols] - dot3(high[block_of(last), at], low[block_of(last), at], uh, ul, 0, 0)
        after = jnp.minimum(k + 1, NG - 1)
        there = block_of(after)
        nxt[:, cols] = diag_rows(after, begin) - dot3(
            high[0:depth, there], low[0:depth, there], high[0:depth, cols], low[0:depth, cols], 0, 0
        )
        nh, nl = split(w)
        wh[k] = nh
        wl[k] = nl
        bh, bl = split(acc[:, there])
        vh, vl = split(dot3(nh, nl, bh, bl, 1, 0))
        now[...] = nxt[:, there] - dot3(vh, vl, vh, vl, 0, 0)

    def side(i, depth):
        at = block_of(i)
        padded = jnp.concatenate([cross[i], jnp.zeros((B - COLS, B), F32)], axis=0).T
        start = jnp.concatenate([side_rows[i].reshape(B, GC), padded], axis=1)
        done = dot3(high[0:depth, at], low[0:depth, at], xh[0:depth, :], xl[0:depth, :], 0, 0)
        sh, sl = split(start - done)
        u = dot3(wh[i], wl[i], sh, sl, 1, 0)
        uh, ul = split(u)
        xh[at, :] = uh
        xl[at, :] = ul
        factor_ref[:, at] = u[:, 0:GC].T[0:ROWS, :]

    def first(k, carry):
        across(k + 2)
        complete(k + 1)

        @pl.when(k == 0)
        def _():
            side_rows[z, y] = summed(PICK)
            for d in range(1, NZ):
                cz(d).start()
            cross[g] = summed(CROSS)
            for d in range(1, NX):
                ex(d).start()
            ep(0).start()

        @pl.when(k == 2)
        def _():
            for zz in range(NZ):
                arrived(zz, None, cz_recv, side_rows)
                for d in range(1, NY):
                    cy(zz, d).start()
            for d in range(1, NX):
                ex(d).wait_recv()
                ep(d).start()

        block(k, 0, 4 * B)
        return carry

    def here(i):
        for d in range(1, NY):
            cy(i, d).wait_recv()

    def second(k, carry):
        across(k + 2)
        complete(k + 1)
        i = 2 * (k - 4)
        here(i)
        here(i + 1)
        block(k, 3, 5 * B)
        side(i, 4 * B)
        side(i + 1, 4 * B)
        return carry

    def third(k, carry):
        @pl.when(k < NG - 1)
        def _():
            complete(k + 1)

        here(k - 2)
        block(k, 5, 7 * B)
        side(k - 2, 6 * B)
        return carry

    lax.fori_loop(0, 4, first, 0)
    for d in range(NX):
        ep(d).wait_recv()
    lax.fori_loop(4, 6, second, 0)
    lax.fori_loop(6, NG, third, 0)
    here(NG - 2)
    here(NG - 1)
    side(NG - 2, 6 * B)
    side(NG - 1, 7 * B)
    drop = dot3(xh[:, GC:], xl[:, GC:], xh[:, 0:GC], xl[:, 0:GC], 0, 0)
    trail_ref[...] = (summed(REST) - drop[0:COLS, :])[:, 0:ROWS]

    finish()
    for d in range(1, NY):
        for p in range(4):
            rs(p, d).wait_send()
        for zz in range(NZ):
            dy(zz, d).wait_send()
            cy(zz, d).wait_send()
    for d in range(1, NZ):
        dz(d).wait_send()
        cz(d).wait_send()
    for d in range(NX):
        for zz in range(NZ):
            if d:
                dx(zz, d).wait_send()
            dp(zz, d).wait_send()
        if d:
            ex(d).wait_send()
        ep(d).wait_send()


def shards(
    tx_fields, rx_fields, layer_of_cell, layer_cond, tx_of_row, rx_of_row, damping, panel_order
):
    lists = [
        jnp.pad(v, (0, LINES * 128 - M)).reshape(LINES, 128)
        for v in (tx_of_row, rx_of_row, damping, panel_order)
    ]
    vmem = pl.BlockSpec(memory_space=VMEM)
    smem = pl.BlockSpec(memory_space=pltpu.SMEM)
    trailing, factor = pl.pallas_call(
        step_kernel,
        out_shape=(
            jax.ShapeDtypeStruct((COLS, ROWS), F32),
            jax.ShapeDtypeStruct((ROWS, PICKED), F32),
        ),
        in_specs=[vmem, vmem, vmem, smem, vmem, vmem, vmem, vmem],
        out_specs=(vmem, vmem),
        scratch_shapes=[
            VMEM((NY, LEFT, RIGHT), F32),
            VMEM((LEFT, RIGHT), F32),
            VMEM((NZ, NCORE, MSGS, 32, CELLS), BF16),
            VMEM((NZ, 1, CELLS), F32),
            VMEM((RIGHT + NY * LEFT, CELLS), BF16),
            VMEM((RIGHT + NY * LEFT, 128), BF16),
            VMEM((RIGHT + NY * LEFT, 128), BF16),
        ]
        + [DMA((NZ, MSGS))] * 2
        + [DMA((NZ,))] * 2
        + [DMA((NZ, MSGS))] * 2
        + [DMA((NCORE, MSGS))]
        + [
            VMEM((B, B), F32),
            VMEM((B, PICKED), F32),
            VMEM((B, PICKED), F32),
            VMEM((PICKED, PICKED), BF16),
            VMEM((PICKED, PICKED), BF16),
            VMEM((NG, B, B), BF16),
            VMEM((NG, B, B), BF16),
            VMEM((PICKED, SIDE), BF16),
            VMEM((PICKED, SIDE), BF16),
            VMEM((NY - 1, LEFT, RIGHT), F32),
            VMEM((NG, NZ, NY, PT, PG), F32),
            VMEM((NZ, NY, PT, GC), F32),
            VMEM((NG, COLS, PG), F32),
        ]
        + [DMA((4, NY))] * 2
        + [DMA((NZ,))] * 2
        + [DMA((NZ, NY))] * 2
        + [DMA((NZ, NX))] * 4
        + [DMA((NZ,))] * 2
        + [DMA((NZ, NY))] * 2
        + [DMA((NX,))] * 4,
        compiler_params=pltpu.CompilerParams(
            collective_id=0, has_side_effects=True, vmem_limit_bytes=34 << 20
        ),
        name="step",
    )(
        tx_fields, rx_fields, layer_of_cell.reshape(-1, 128), layer_cond, *lists,
    )
    return trailing.T, factor


def solution(mesh):
    placed = (P(None, "tile"), P(None, "tile"), P("tile"), P(), P(), P(), P(), P())
    return jax.shard_map(
        shards,
        mesh=mesh,
        in_specs=placed,
        out_specs=(P("grp", "tile"), P("grp", None)),
        check_vma=False,
    )
```

```python
import functools

import jax
import jax.numpy as jnp
from jax import lax
from jax.experimental import pallas as pl
from jax.experimental.pallas import tpu as pltpu
from jax.sharding import PartitionSpec as P

F32 = jnp.float32
BF16 = jnp.bfloat16
MESH = pl.DeviceIdType.MESH
VMEM = pltpu.VMEM
DMA = pltpu.SemaphoreType.DMA

M = 2816
NCELLS = 32768
PICKED = 1024
NX, NY, NZ, NCORE = 4, 4, 8, 2
NG = NX * NCORE
NT = NY * NZ
ROWS = M // NG
COLS = M // NT
PG = PICKED // NG
PT = PICKED // NT
CELLS = NCELLS // NT
RIGHT = 512
LEFT = COLS + PT
B = 128
GC = RIGHT - PG


def dot(a, b, ca, cb):
    return lax.dot_general(a, b, (((ca,), (cb,)), ((), ())), preferred_element_type=F32)


def split(x):
    hi = x.astype(BF16)
    return hi, (x - hi.astype(F32)).astype(BF16)


def places():
    g = lax.axis_index("grp")
    t = lax.axis_index("tile")
    return g // NCORE, g % NCORE, t // NY, t % NY


def at_z(z, y):
    return {"tile": lax.rem(z + NZ, NZ) * NY + y}


def greet(peers):
    barrier = pltpu.get_barrier_semaphore()
    for peer in peers:
        pl.semaphore_signal(barrier, inc=1, device_id=peer, device_id_type=MESH)
    pl.semaphore_wait(barrier, len(peers))


def sends(src, dst, send, recv, peer):
    return pltpu.make_async_remote_copy(
        src_ref=src, dst_ref=dst, send_sem=send, recv_sem=recv, device_id=peer, device_id_type=MESH
    )


def owner_of(z, i):
    hops = (i + 1) // 2
    return lax.rem(z + NZ + jnp.where(i % 2 == 1, -hops, hops), NZ)


MSGS = 3
LINES = 24


def look_up(ids, tables):
    count = ids.shape[0]
    lanes = lax.broadcasted_iota(jnp.int32, (count, 128), 1)
    line = jnp.where((ids >> 7) == lanes, 1.0, 0.0).astype(BF16)[:, 0:LINES]
    found = dot(line, jnp.concatenate(tables, axis=1).astype(BF16), 1, 0)
    mine = (ids & 127) == lanes
    return [
        jnp.sum(jnp.where(mine, found[:, 128 * i : 128 * i + 128], 0.0), axis=1, keepdims=True)
        for i in range(len(tables))
    ]


def column(row):
    at = [lax.broadcasted_iota(jnp.int32, (128, 128), d) for d in (0, 1)]
    return jnp.sum(jnp.where(at[0] == at[1], row, 0.0), axis=1, keepdims=True)


def prepare(tx_list, rx_list, damp_list, order, tx_hot, rx_hot, damp, g, z, y, t):
    def run(begin, count):
        return begin + lax.broadcasted_iota(jnp.int32, (count, 1), 0)

    right_row = order[pl.ds(g, 1), :].astype(F32)
    left_picks = column(order[pl.ds(z, 1), :].astype(F32)).astype(jnp.int32)
    ids = [column(right_row).astype(jnp.int32), run(g * ROWS, ROWS), run(0, RIGHT - PG - ROWS) * 0 - 1]
    for j in range(NY):
        ids += [run((z * NY + j) * COLS, COLS), left_picks[PT * j : PT * j + PT, :]]
    ids = jnp.concatenate(ids, axis=0)
    txv, rxv = look_up(ids, [v[...].astype(F32) for v in (tx_list, rx_list)])
    none = jnp.where(ids < 0, -1.0, 0.0)
    lane = lax.broadcasted_iota(jnp.int32, (RIGHT + NY * LEFT, 128), 1).astype(F32)
    tx_hot[...] = jnp.where(txv + none == lane, 1.0, 0.0).astype(BF16)
    rx_hot[...] = jnp.where(rxv + none == lane, 1.0, 0.0).astype(BF16)

    own_picks = sum(jnp.where(y == j, left_picks[PT * j : PT * j + PT, :], 0) for j in range(NY))
    left = jnp.concatenate([run(t * COLS, COLS), own_picks], axis=0)
    table = damp_list[...]
    high = table.astype(BF16).astype(F32)
    mid = (table - high).astype(BF16).astype(F32)
    terms = look_up(left, [high, mid, table - high - mid])
    near = terms[0] + (terms[1] + terms[2])
    natural = lax.broadcasted_iota(jnp.int32, (1, GC), 1)
    natural = jnp.where(natural < ROWS, g * ROWS + natural, -1)
    right = jnp.concatenate([right_row.astype(jnp.int32), natural], axis=1)
    damp[...] = jnp.where(left == right, near, 0.0)


def gram_part(
    tx_ref, rx_ref, layer_ref, cond_ref, prep, part, layers, held, conds, sens, tx_hot, rx_hot,
    ring_send, ring_recv, cond_send, cond_recv, pair_send, pair_recv, local,
):
    x, c, z, y = places()
    up, down, pair = at_z(z + 1, y), at_z(z + NZ - 1, y), {"grp": x * NCORE + 1 - c}

    def own(m):
        if m == 0:
            return tx_ref.at[pl.ds(pl.multiple_of(c * 32, 32), 32), :]
        return rx_ref.at[pl.ds(pl.multiple_of(c * 64 + (m - 1) * 32, 32), 32), :]

    def way(i, m):
        return i % 2 == 1 if i < NZ - 1 else m == 0

    def ring(i, m):
        first = i < 3
        rising = way(i, m)
        prior = i - 2 if i < NZ - 1 or rising else i - 1
        o = z if first else owner_of(z, prior)
        src = own(m) if first else held.at[o, c, m]
        return sends(src, held.at[o, c, m], ring_send.at[i, m], ring_recv.at[i, m], up if rising else down)

    def line(i):
        o = z if i < 3 else owner_of(z, i - 2)
        return sends(conds.at[o], conds.at[o], cond_send.at[i], cond_recv.at[i], up if i % 2 == 1 else down)

    def to_pair(i, m):
        o = owner_of(z, i)
        return sends(held.at[o, c, m], held.at[o, c, m], pair_send.at[i, m], pair_recv.at[i, m], pair)

    def arrive(i, m):
        ring(i, m).wait_recv()
        if i < NZ - 3:
            ring(i + 2, m).start()
        elif i < NZ - 1 and way(NZ - 1, m) == (i % 2 == 1):
            ring(NZ - 1, m).start()
        to_pair(i, m).start()
        if m == 0:
            line(i).wait_recv()
            if i + 2 < NZ:
                line(i + 2).start()

    for m in range(MSGS):
        ring(1, m).start()
        ring(2, m).start()
    mine = []
    for core in range(NCORE):
        mine.append(pltpu.make_async_copy(tx_ref.at[32 * core : 32 * core + 32, :], held.at[z, core, 0], local.at[core, 0]))
        for m in (1, 2):
            at = 64 * core + 32 * (m - 1)
            mine.append(pltpu.make_async_copy(rx_ref.at[at : at + 32, :], held.at[z, core, m], local.at[core, m]))
    mine.append(pltpu.make_async_copy(layer_ref, layers, local.at[0, MSGS]))
    for copy in mine:
        copy.start()
    mine.pop().wait()
    layer = layers[...]
    cond = jnp.zeros(layer.shape, F32)
    for level in range(32):
        cond = jnp.where(layer == level, cond_ref[level], cond)
    conds[z] = jnp.concatenate([cond[r : r + 1, :] for r in range(CELLS // 128)], axis=1)
    line(1).start()
    line(2).start()
    prep()
    part[...] = jnp.zeros_like(part)
    for copy in mine:
        copy.wait()
    for m in range(MSGS):
        arrive(1, m)

    def body(i, carry):
        for n in range(NZ - 1):
            @pl.when(i == n)
            def _():
                for m in range(MSGS):
                    if n + 2 < NZ - 1:
                        arrive(n + 2, m)
                    elif way(NZ - 1, m) == (n % 2 == 1):
                        arrive(NZ - 1, m)

        for n in range(1, NZ):
            @pl.when(i == n)
            def _():
                for m in range(MSGS):
                    to_pair(n, m).wait_recv()

        o = owner_of(z, i)
        txs = jnp.concatenate([held[o, k, 0] for k in range(NCORE)], axis=0)
        rxs = jnp.concatenate([held[o, k, m] for k in range(NCORE) for m in (1, 2)], axis=0)
        both = dot(tx_hot[:, 0:64], txs, 1, 0) * dot(rx_hot[...], rxs, 1, 0)
        sens[...] = (both * conds[o]).astype(BF16)
        part[...] += dot(sens[RIGHT:, :], sens[0:RIGHT, :], 1, 1).reshape(NY, LEFT, RIGHT)
        return carry

    lax.fori_loop(0, NZ, body, 0)

    def finish():
        for i in range(1, NZ):
            for m in range(MSGS):
                ring(i, m).wait_send()
                to_pair(i, m).wait_send()
            line(i).wait_send()

    return finish


def tree(vs):
    while len(vs) > 1:
        vs = [vs[i] + vs[i + 1] if i + 1 < len(vs) else vs[i] for i in range(0, len(vs), 2)]
    return vs[0]


def inverse_factor(m):
    W = 16
    H = W // 8
    lane = lax.broadcasted_iota(jnp.int32, (8, B), 1)
    sub = lax.broadcasted_iota(jnp.int32, (8, B), 0)
    tiles = [m[8 * i : 8 * i + 8, :] for i in range(B // 8)]
    full = lambda v: jnp.broadcast_to(v, (8, B))
    column = lambda t, j: jnp.take_along_axis(t, jnp.full((8, B), j, jnp.int32), axis=1)
    for j in range(0, B, W):
        q = j // 8
        here = (lane >= j) & (lane < j + W)
        cs = {}
        for p in range(W):
            for h in range(p // 8, H):
                cs[p, h] = column(tiles[q + h], j + p)
        rows = [
            jnp.where(lane == j + 8 * h + sub, 1.0, jnp.where(here, 0.0, tiles[q + h])) for h in range(H)
        ]
        pivots, begun, low, fixes = {}, [None] * W, {}, []
        for p in range(0, W, 2):
            hp, s = divmod(p, 8)
            c0, c1 = cs[p, hp], cs[p + 1, hp]
            a, b, c = full(c0[s : s + 1, :]), full(c0[s + 1 : s + 2, :]), full(c1[s + 1 : s + 2, :])
            r = 1.0 / (a * c - b * b)
            ar, br, cr = a * r, b * r, c * r
            ratio = b / a
            pivots[p], pivots[p + 1] = a, c - b * ratio
            for k in range(p + 2, W):
                e0 = full(cs[p, k // 8][k % 8 : k % 8 + 1, :])
                e1 = full(cs[p + 1, k // 8][k % 8 : k % 8 + 1, :])
                low[k, p] = cr * e0 - br * e1
                low[k, p + 1] = ar * e1 - br * e0
                for h in range(k // 8, H):
                    cs[k, h] = cs[k, h] - (cs[p, h] * low[k, p] + cs[p + 1, h] * low[k, p + 1])
            r0, r1 = full(rows[hp][s : s + 1, :]), full(rows[hp][s + 1 : s + 2, :])
            x0, x1 = cr * r0 - br * r1, ar * r1 - br * r0
            begun[p], begun[p + 1] = x0, x1
            fixes.append((hp, s, ratio * r0))
            for h in range(hp, H):
                if h == hp and s == 6:
                    continue
                f0, f1 = cs[p, h], cs[p + 1, h]
                if h == hp:
                    f0, f1 = jnp.where(sub > s + 1, f0, 0.0), jnp.where(sub > s + 1, f1, 0.0)
                rows[h] = rows[h] - (f0 * x0 + f1 * x1)
        back = [None] * W
        for p in reversed(range(W)):
            v = begun[p]
            for i in reversed(range(p // 2 * 2 + 2, W)):
                v = v - low[i, p] * back[i]
            back[p] = v
        far = q + 2 * H
        for i in range(q + H, min(far, B // 8)):
            terms = [column(tiles[i], j + p) * back[p] for p in range(W)]
            tiles[i] = jnp.where(here, 0.0, tiles[i]) - tree(terms)
        if far < B // 8:
            packed = []
            for h in range(H):
                v = back[8 * h]
                for s in range(1, 8):
                    v = jnp.where(sub == s, back[8 * h + s], v)
                packed.append(v)
            zh, zl = split(jnp.concatenate(tiles[far:], axis=0)[:, j : j + W])
            ph, pq = split(jnp.concatenate(packed, axis=0))
            drop = dot3(zh, zl, ph, pq, 1, 0)
            for i in range(far, B // 8):
                k = 8 * (i - far)
                tiles[i] = jnp.where(here, 0.0, tiles[i]) - drop[k : k + 8, :]
        for h, s, fix in fixes:
            rows[h] = jnp.where(sub == s + 1, rows[h] - fix, rows[h])
        for h in range(H):
            scale = pivots[8 * h]
            for s in range(1, 8):
                scale = jnp.where(sub == s, pivots[8 * h + s], scale)
            tiles[q + h] = rows[h] * lax.rsqrt(scale)
    w = jnp.concatenate(tiles, axis=0)
    r = lax.broadcasted_iota(jnp.int32, (B, B), 0)
    c = lax.broadcasted_iota(jnp.int32, (B, B), 1)
    return jnp.where(r >= c, w, 0.0)


SIDE = GC + B


def dot3(ah, al, bh, bl, ca, cb):
    return dot(ah, bh, ca, cb) + (dot(ah, bl, ca, cb) + dot(al, bh, ca, cb))


def block_of(k):
    return pl.ds(pl.multiple_of(k * B, B), B)


DIAG, PICK, CROSS, REST = 0, 1, 2, 3
PARTS = (
    (slice(COLS, LEFT), slice(0, PG)),
    (slice(COLS, LEFT), slice(PG, RIGHT)),
    (slice(0, COLS), slice(0, PG)),
    (slice(0, COLS), slice(PG, RIGHT)),
)


def step_kernel(
    tx_ref, rx_ref, layer_ref, cond_ref, tx_list, rx_list, damp_list, order,
    trail_ref, factor_ref,
    part_ref, damp_ref, layers, held, conds, sens, tx_hot, rx_hot,
    gr_send, gr_recv, gc_send, gc_recv, gp_send, gp_recv, local,
    now, acc, nxt, high, low, wh, wl, xh, xl, got, diag, side_rows, cross,
    rs_send, rs_recv, dz_send, dz_recv, dy_send, dy_recv, dx_send, dx_recv, dp_send, dp_recv,
    cz_send, cz_recv, cy_send, cy_recv, ex_send, ex_recv, ep_send, ep_recv,
):
    x, c, z, y = places()
    g = x * NCORE + c
    pair = {"grp": x * NCORE + 1 - c}
    at_y = [None] + [{"tile": z * NY + lax.rem(y + d, NY)} for d in range(1, NY)]
    at_x = [None] + [{"grp": lax.rem(x + d, NX) * NCORE + c} for d in range(1, NX)]
    in_z = [None] + [{"tile": lax.rem(z + d, NZ) * NY + y} for d in range(1, NZ)]
    greet(at_y[1:] + at_x[1:] + in_z[1:] + [pair])

    def prep():
        prepare(tx_list, rx_list, damp_list, order, tx_hot, rx_hot, damp_ref, g, z, y, z * NY + y)

    finish = gram_part(
        tx_ref, rx_ref, layer_ref, cond_ref, prep, part_ref, layers, held, conds, sens, tx_hot, rx_hot,
        gr_send, gr_recv, gc_send, gc_recv, gp_send, gp_recv, local,
    )

    def rs(p, d):
        rows, cols = PARTS[p]
        return sends(
            part_ref.at[lax.rem(y + d, NY), rows, cols], got.at[d - 1, rows, cols],
            rs_send.at[p, d], rs_recv.at[p, d], at_y[d],
        )

    def start_sums(p):
        for d in range(1, NY):
            rs(p, d).start()

    def summed(p):
        rows, cols = PARTS[p]
        total = part_ref[y, rows, cols]
        for d in range(1, NY):
            rs(p, d).wait_recv()
            total += got[d - 1, rows, cols]
        return total * (1.0 / NCELLS) + damp_ref[rows, cols]

    def dz(d):
        return sends(diag.at[g, z, y], diag.at[g, z, y], dz_send.at[d], dz_recv.at[d], in_z[d])

    def dy(zz, d):
        return sends(diag.at[g, zz, y], diag.at[g, zz, y], dy_send.at[zz, d], dy_recv.at[zz, d], at_y[d])

    def dx(zz, d):
        return sends(diag.at[g, zz], diag.at[g, zz], dx_send.at[zz, d], dx_recv.at[zz, d], at_x[d])

    def dp(zz, d):
        gd = lax.rem(x + NX - d, NX) * NCORE + c
        return sends(diag.at[gd, zz], diag.at[gd, zz], dp_send.at[zz, d], dp_recv.at[zz, d], pair)

    def cz(d):
        return sends(side_rows.at[z, y], side_rows.at[z, y], cz_send.at[d], cz_recv.at[d], in_z[d])

    def cy(zz, d):
        return sends(side_rows.at[zz, y], side_rows.at[zz, y], cy_send.at[zz, d], cy_recv.at[zz, d], at_y[d])

    def ex(d):
        return sends(cross.at[g], cross.at[g], ex_send.at[d], ex_recv.at[d], at_x[d])

    def ep(d):
        gd = lax.rem(x + NX - d, NX) * NCORE + c
        return sends(cross.at[gd], cross.at[gd], ep_send.at[d], ep_recv.at[d], pair)

    def arrived(zz, copy, sem_recv, ref):
        d = lax.rem(z + NZ - zz, NZ)

        @pl.when(d != 0)
        def _():
            sends(ref.at[zz, y], ref.at[zz, y], sem_recv.at[d], sem_recv.at[d], pair).wait_recv()

    def across(zz):
        for d in range(1, NX):
            dx(zz, d).wait_recv()
            dp(zz, d).start()

    def complete(zz):
        for d in range(NX):
            dp(zz, d).wait_recv()

    start_sums(DIAG)
    high[...] = jnp.zeros_like(high)
    low[...] = jnp.zeros_like(low)
    xh[...] = jnp.zeros_like(xh)
    xl[...] = jnp.zeros_like(xl)
    acc[...] = jnp.zeros_like(acc)
    wh[0] = jnp.zeros((B, B), BF16)
    wl[0] = jnp.zeros((B, B), BF16)
    diag[g, z, y] = summed(DIAG)
    for d in range(1, NZ):
        dz(d).start()
    for zz in range(NZ):
        arrived(zz, None, dz_recv, diag.at[g])
        for d in range(1, NY):
            dy(zz, d).start()
    for zz in range(NZ):
        for d in range(1, NY):
            dy(zz, d).wait_recv()
        for d in range(1, NX):
            dx(zz, d).start()
        dp(zz, 0).start()
    start_sums(PICK)
    start_sums(CROSS)
    start_sums(REST)
    across(0)
    across(1)
    complete(0)

    def diag_rows(k, begin):
        return jnp.concatenate([diag[i, k].reshape(B, B) for i in range(begin, NG)], axis=1)

    nxt[...] = diag_rows(0, 0)
    now[...] = diag[0, 0].reshape(B, B)

    def block(k, begin, depth):
        w = inverse_factor(now[...])
        last = jnp.maximum(k - 1, 0)
        cols = slice(begin * B, PICKED)
        ah, al = split(acc[:, cols])
        uh, ul = split(dot3(wh[last], wl[last], ah, al, 1, 0))
        high[block_of(last), cols] = uh
        low[block_of(last), cols] = ul
        at = block_of(k)
        acc[:, cols] = nxt[:, cols] - dot3(high[block_of(last), at], low[block_of(last), at], uh, ul, 0, 0)
        after = jnp.minimum(k + 1, NG - 1)
        there = block_of(after)
        nxt[:, cols] = diag_rows(after, begin) - dot3(
            high[0:depth, there], low[0:depth, there], high[0:depth, cols], low[0:depth, cols], 0, 0
        )
        nh, nl = split(w)
        wh[k] = nh
        wl[k] = nl
        bh, bl = split(acc[:, there])
        vh, vl = split(dot3(nh, nl, bh, bl, 1, 0))
        now[...] = nxt[:, there] - dot3(vh, vl, vh, vl, 0, 0)

    def side(i, depth):
        at = block_of(i)
        padded = jnp.concatenate([cross[i], jnp.zeros((B - COLS, B), F32)], axis=0).T
        start = jnp.concatenate([side_rows[i].reshape(B, GC), padded], axis=1)
        done = dot3(high[0:depth, at], low[0:depth, at], xh[0:depth, :], xl[0:depth, :], 0, 0)
        sh, sl = split(start - done)
        u = dot3(wh[i], wl[i], sh, sl, 1, 0)
        uh, ul = split(u)
        xh[at, :] = uh
        xl[at, :] = ul
        factor_ref[:, at] = u[:, 0:GC].T[0:ROWS, :]

    def first(k, carry):
        across(k + 2)
        complete(k + 1)

        @pl.when(k == 0)
        def _():
            side_rows[z, y] = summed(PICK)
            for d in range(1, NZ):
                cz(d).start()
            cross[g] = summed(CROSS)
            for d in range(1, NX):
                ex(d).start()
            ep(0).start()

        @pl.when(k == 2)
        def _():
            for zz in range(NZ):
                arrived(zz, None, cz_recv, side_rows)
                for d in range(1, NY):
                    cy(zz, d).start()
            for d in range(1, NX):
                ex(d).wait_recv()
                ep(d).start()

        block(k, 0, 4 * B)
        return carry

    def here(i):
        for d in range(1, NY):
            cy(i, d).wait_recv()

    def second(k, carry):
        across(k + 2)
        complete(k + 1)
        i = 2 * (k - 4)
        here(i)
        here(i + 1)
        block(k, 3, 5 * B)
        side(i, 4 * B)
        side(i + 1, 4 * B)
        return carry

    def third(k, carry):
        @pl.when(k < NG - 1)
        def _():
            complete(k + 1)

        here(k - 2)
        block(k, 5, 7 * B)
        side(k - 2, 6 * B)
        return carry

    lax.fori_loop(0, 4, first, 0)
    for d in range(NX):
        ep(d).wait_recv()
    lax.fori_loop(4, 6, second, 0)
    lax.fori_loop(6, NG, third, 0)
    here(NG - 2)
    here(NG - 1)
    side(NG - 2, 6 * B)
    side(NG - 1, 7 * B)
    drop = dot3(xh[:, GC:], xl[:, GC:], xh[:, 0:GC], xl[:, 0:GC], 0, 0)
    trail_ref[...] = (summed(REST) - drop[0:COLS, :])[:, 0:ROWS]

    finish()
    for d in range(1, NY):
        for p in range(4):
            rs(p, d).wait_send()
        for zz in range(NZ):
            dy(zz, d).wait_send()
            cy(zz, d).wait_send()
    for d in range(1, NZ):
        dz(d).wait_send()
        cz(d).wait_send()
    for d in range(NX):
        for zz in range(NZ):
            if d:
                dx(zz, d).wait_send()
            dp(zz, d).wait_send()
        if d:
            ex(d).wait_send()
        ep(d).wait_send()


def shards(
    tx_fields, rx_fields, layer_of_cell, layer_cond, tx_of_row, rx_of_row, damping, panel_order
):
    lists = [
        jnp.pad(v, (0, LINES * 128 - M)).reshape(LINES, 128)
        for v in (tx_of_row, rx_of_row, damping, panel_order)
    ]
    vmem = pl.BlockSpec(memory_space=VMEM)
    smem = pl.BlockSpec(memory_space=pltpu.SMEM)
    hbm = pl.BlockSpec(memory_space=pltpu.HBM)
    trailing, factor = pl.pallas_call(
        step_kernel,
        out_shape=(
            jax.ShapeDtypeStruct((COLS, ROWS), F32),
            jax.ShapeDtypeStruct((ROWS, PICKED), F32),
        ),
        in_specs=[hbm, hbm, hbm, smem, vmem, vmem, vmem, vmem],
        out_specs=(vmem, vmem),
        scratch_shapes=[
            VMEM((NY, LEFT, RIGHT), F32),
            VMEM((LEFT, RIGHT), F32),
            VMEM((CELLS // 128, 128), jnp.int32),
            VMEM((NZ, NCORE, MSGS, 32, CELLS), BF16),
            VMEM((NZ, 1, CELLS), F32),
            VMEM((RIGHT + NY * LEFT, CELLS), BF16),
            VMEM((RIGHT + NY * LEFT, 128), BF16),
            VMEM((RIGHT + NY * LEFT, 128), BF16),
        ]
        + [DMA((NZ, MSGS))] * 2
        + [DMA((NZ,))] * 2
        + [DMA((NZ, MSGS))] * 2
        + [DMA((NCORE, MSGS + 1))]
        + [
            VMEM((B, B), F32),
            VMEM((B, PICKED), F32),
            VMEM((B, PICKED), F32),
            VMEM((PICKED, PICKED), BF16),
            VMEM((PICKED, PICKED), BF16),
            VMEM((NG, B, B), BF16),
            VMEM((NG, B, B), BF16),
            VMEM((PICKED, SIDE), BF16),
            VMEM((PICKED, SIDE), BF16),
            VMEM((NY - 1, LEFT, RIGHT), F32),
            VMEM((NG, NZ, NY, PT, PG), F32),
            VMEM((NZ, NY, PT, GC), F32),
            VMEM((NG, COLS, PG), F32),
        ]
        + [DMA((4, NY))] * 2
        + [DMA((NZ,))] * 2
        + [DMA((NZ, NY))] * 2
        + [DMA((NZ, NX))] * 4
        + [DMA((NZ,))] * 2
        + [DMA((NZ, NY))] * 2
        + [DMA((NX,))] * 4,
        compiler_params=pltpu.CompilerParams(
            collective_id=0, has_side_effects=True, vmem_limit_bytes=34 << 20
        ),
        name="step",
    )(
        *(
            pltpu.with_memory_space_constraint(v, pltpu.HBM)
            for v in (tx_fields, rx_fields, layer_of_cell.reshape(-1, 128))
        ),
        layer_cond,
        *lists,
    )
    return trailing.T, factor


def solution(mesh):
    placed = (P(None, "tile"), P(None, "tile"), P("tile"), P(), P(), P(), P(), P())
    return jax.shard_map(
        shards,
        mesh=mesh,
        in_specs=placed,
        out_specs=(P("grp", "tile"), P("grp", None)),
        check_vma=False,
    )
```

```python
import functools

import jax
import jax.numpy as jnp
from jax import lax
from jax.experimental import pallas as pl
from jax.experimental.pallas import tpu as pltpu
from jax.sharding import PartitionSpec as P

F32 = jnp.float32
BF16 = jnp.bfloat16
MESH = pl.DeviceIdType.MESH
VMEM = pltpu.VMEM
DMA = pltpu.SemaphoreType.DMA

M = 2816
NCELLS = 32768
PICKED = 1024
NX, NY, NZ, NCORE = 4, 4, 8, 2
NG = NX * NCORE
NT = NY * NZ
ROWS = M // NG
COLS = M // NT
PG = PICKED // NG
PT = PICKED // NT
CELLS = NCELLS // NT
RIGHT = 512
LEFT = COLS + PT
B = 128
GC = RIGHT - PG


def dot(a, b, ca, cb):
    return lax.dot_general(a, b, (((ca,), (cb,)), ((), ())), preferred_element_type=F32)


def split(x):
    hi = x.astype(BF16)
    return hi, (x - hi.astype(F32)).astype(BF16)


def places():
    g = lax.axis_index("grp")
    t = lax.axis_index("tile")
    return g // NCORE, g % NCORE, t // NY, t % NY


def at_z(z, y):
    return {"tile": lax.rem(z + NZ, NZ) * NY + y}


def greet(peers):
    barrier = pltpu.get_barrier_semaphore()
    for peer in peers:
        pl.semaphore_signal(barrier, inc=1, device_id=peer, device_id_type=MESH)
    pl.semaphore_wait(barrier, len(peers))


def sends(src, dst, send, recv, peer):
    return pltpu.make_async_remote_copy(
        src_ref=src, dst_ref=dst, send_sem=send, recv_sem=recv, device_id=peer, device_id_type=MESH
    )


def owner_of(z, i):
    hops = (i + 1) // 2
    return lax.rem(z + NZ + jnp.where(i % 2 == 1, -hops, hops), NZ)


MSGS = 3
LINES = 24


def look_up(ids, tables):
    count = ids.shape[0]
    lanes = lax.broadcasted_iota(jnp.int32, (count, 128), 1)
    line = jnp.where((ids >> 7) == lanes, 1.0, 0.0).astype(BF16)[:, 0:LINES]
    found = dot(line, jnp.concatenate(tables, axis=1).astype(BF16), 1, 0)
    mine = (ids & 127) == lanes
    return [
        jnp.sum(jnp.where(mine, found[:, 128 * i : 128 * i + 128], 0.0), axis=1, keepdims=True)
        for i in range(len(tables))
    ]


def column(row):
    at = [lax.broadcasted_iota(jnp.int32, (128, 128), d) for d in (0, 1)]
    return jnp.sum(jnp.where(at[0] == at[1], row, 0.0), axis=1, keepdims=True)


def prepare(
    tx_list, rx_list, damp_list, order, tx_hot, rx_hot, tx_pick, rx_pick, damp, g, z, y, t
):
    def run(begin, count):
        return begin + lax.broadcasted_iota(jnp.int32, (count, 1), 0)

    right_row = order[pl.ds(g, 1), :].astype(F32)
    left_picks = column(order[pl.ds(z, 1), :].astype(F32)).astype(jnp.int32)
    ids = [column(right_row).astype(jnp.int32), run(g * ROWS, ROWS), run(0, RIGHT - PG - ROWS) * 0 - 1]
    for j in range(NY):
        ids += [run((z * NY + j) * COLS, COLS), left_picks[PT * j : PT * j + PT, :]]
    ids = jnp.concatenate(ids, axis=0)
    txv, rxv = look_up(ids, [v[...].astype(F32) for v in (tx_list, rx_list)])
    none = jnp.where(ids < 0, -1.0, 0.0)
    lane = lax.broadcasted_iota(jnp.int32, (RIGHT + NY * LEFT, 128), 1).astype(F32)
    tx_hot[...] = jnp.where(txv + none == lane, 1.0, 0.0).astype(BF16)
    rx_hot[...] = jnp.where(rxv + none == lane, 1.0, 0.0).astype(BF16)
    picks = jnp.concatenate([ids[0:PG, :], left_picks], axis=0)
    txv, rxv = look_up(picks, [v[...].astype(F32) for v in (tx_list, rx_list)])
    tx_pick[...] = jnp.where(txv == lane[0 : 2 * PG, :], 1.0, 0.0).astype(BF16)
    rx_pick[...] = jnp.where(rxv == lane[0 : 2 * PG, :], 1.0, 0.0).astype(BF16)

    own_picks = sum(jnp.where(y == j, left_picks[PT * j : PT * j + PT, :], 0) for j in range(NY))
    left = jnp.concatenate([run(t * COLS, COLS), own_picks], axis=0)
    table = damp_list[...]
    high = table.astype(BF16).astype(F32)
    mid = (table - high).astype(BF16).astype(F32)
    terms = look_up(left, [high, mid, table - high - mid])
    near = terms[0] + (terms[1] + terms[2])
    natural = lax.broadcasted_iota(jnp.int32, (1, GC), 1)
    natural = jnp.where(natural < ROWS, g * ROWS + natural, -1)
    right = jnp.concatenate([right_row.astype(jnp.int32), natural], axis=1)
    damp[...] = jnp.where(left == right, near, 0.0)


def gram_part(
    tx_ref, rx_ref, layer_ref, cond_ref, prep, part, diag_part, layers, held, conds, sens,
    tx_hot, rx_hot, tx_pick, rx_pick,
    ring_send, ring_recv, cond_send, cond_recv, pair_send, pair_recv, local,
):
    x, c, z, y = places()
    up, down, pair = at_z(z + 1, y), at_z(z + NZ - 1, y), {"grp": x * NCORE + 1 - c}

    def own(m):
        if m == 0:
            return tx_ref.at[pl.ds(pl.multiple_of(c * 32, 32), 32), :]
        return rx_ref.at[pl.ds(pl.multiple_of(c * 64 + (m - 1) * 32, 32), 32), :]

    def way(i, m):
        return i % 2 == 1 if i < NZ - 1 else m == 0

    def ring(i, m):
        first = i < 3
        rising = way(i, m)
        prior = i - 2 if i < NZ - 1 or rising else i - 1
        o = z if first else owner_of(z, prior)
        src = own(m) if first else held.at[o, c, m]
        return sends(src, held.at[o, c, m], ring_send.at[i, m], ring_recv.at[i, m], up if rising else down)

    def line(i):
        o = z if i < 3 else owner_of(z, i - 2)
        return sends(conds.at[o], conds.at[o], cond_send.at[i], cond_recv.at[i], up if i % 2 == 1 else down)

    def to_pair(i, m):
        o = owner_of(z, i)
        return sends(held.at[o, c, m], held.at[o, c, m], pair_send.at[i, m], pair_recv.at[i, m], pair)

    def arrive(i, m):
        ring(i, m).wait_recv()
        if i < NZ - 3:
            ring(i + 2, m).start()
        elif i < NZ - 1 and way(NZ - 1, m) == (i % 2 == 1):
            ring(NZ - 1, m).start()
        to_pair(i, m).start()
        if m == 0:
            line(i).wait_recv()
            if i + 2 < NZ:
                line(i + 2).start()

    for m in range(MSGS):
        ring(1, m).start()
        ring(2, m).start()
    mine = []
    for core in range(NCORE):
        mine.append(pltpu.make_async_copy(tx_ref.at[32 * core : 32 * core + 32, :], held.at[z, core, 0], local.at[core, 0]))
        for m in (1, 2):
            at = 64 * core + 32 * (m - 1)
            mine.append(pltpu.make_async_copy(rx_ref.at[at : at + 32, :], held.at[z, core, m], local.at[core, m]))
    mine.append(pltpu.make_async_copy(layer_ref, layers, local.at[0, MSGS]))
    for copy in mine:
        copy.start()
    mine.pop().wait()
    layer = layers[...]
    cond = jnp.zeros(layer.shape, F32)
    for level in range(32):
        cond = jnp.where(layer == level, cond_ref[level], cond)
    conds[z] = jnp.concatenate([cond[r : r + 1, :] for r in range(CELLS // 128)], axis=1)
    line(1).start()
    line(2).start()
    prep()
    part[...] = jnp.zeros_like(part)
    diag_part[...] = jnp.zeros_like(diag_part)
    for copy in mine:
        copy.wait()
    for m in range(MSGS):
        arrive(1, m)

    def rows_of(o, tx_select, rx_select):
        txs = jnp.concatenate([held[o, k, 0] for k in range(NCORE)], axis=0)
        rxs = jnp.concatenate([held[o, k, m] for k in range(NCORE) for m in (1, 2)], axis=0)
        both = dot(tx_select[:, 0:64], txs, 1, 0) * dot(rx_select[...], rxs, 1, 0)
        return (both * conds[o]).astype(BF16)

    def everything(o):
        sens[...] = rows_of(o, tx_hot, rx_hot)
        part[...] += dot(sens[RIGHT:, :], sens[0:RIGHT, :], 1, 1).reshape(NY, LEFT, RIGHT)

    def body(i, carry):
        for n in range(NZ - 1):
            @pl.when(i == n)
            def _():
                for m in range(MSGS):
                    if n + 2 < NZ - 1:
                        arrive(n + 2, m)
                    elif way(NZ - 1, m) == (n % 2 == 1):
                        arrive(NZ - 1, m)

        for n in range(1, NZ):
            @pl.when(i == n)
            def _():
                for m in range(MSGS):
                    to_pair(n, m).wait_recv()

        o = owner_of(z, i)
        sens_pick = rows_of(o, tx_pick, rx_pick)
        product = dot(sens_pick[PG:, :], sens_pick[0:PG, :], 1, 1)
        diag_part[...] += product.reshape(NY, PT, PG)
        return carry

    lax.fori_loop(0, NZ, body, 0)

    def finish():
        for i in range(1, NZ):
            for m in range(MSGS):
                ring(i, m).wait_send()
                to_pair(i, m).wait_send()
            line(i).wait_send()

    return everything, finish


def tree(vs):
    while len(vs) > 1:
        vs = [vs[i] + vs[i + 1] if i + 1 < len(vs) else vs[i] for i in range(0, len(vs), 2)]
    return vs[0]


def inverse_factor(m):
    W = 16
    H = W // 8
    lane = lax.broadcasted_iota(jnp.int32, (8, B), 1)
    sub = lax.broadcasted_iota(jnp.int32, (8, B), 0)
    tiles = [m[8 * i : 8 * i + 8, :] for i in range(B // 8)]
    full = lambda v: jnp.broadcast_to(v, (8, B))
    column = lambda t, j: jnp.take_along_axis(t, jnp.full((8, B), j, jnp.int32), axis=1)
    for j in range(0, B, W):
        q = j // 8
        here = (lane >= j) & (lane < j + W)
        cs = {}
        for p in range(W):
            for h in range(p // 8, H):
                cs[p, h] = column(tiles[q + h], j + p)
        rows = [
            jnp.where(lane == j + 8 * h + sub, 1.0, jnp.where(here, 0.0, tiles[q + h])) for h in range(H)
        ]
        pivots, begun, low, fixes = {}, [None] * W, {}, []
        for p in range(0, W, 2):
            hp, s = divmod(p, 8)
            c0, c1 = cs[p, hp], cs[p + 1, hp]
            a, b, c = full(c0[s : s + 1, :]), full(c0[s + 1 : s + 2, :]), full(c1[s + 1 : s + 2, :])
            r = 1.0 / (a * c - b * b)
            ar, br, cr = a * r, b * r, c * r
            ratio = b / a
            pivots[p], pivots[p + 1] = a, c - b * ratio
            for k in range(p + 2, W):
                e0 = full(cs[p, k // 8][k % 8 : k % 8 + 1, :])
                e1 = full(cs[p + 1, k // 8][k % 8 : k % 8 + 1, :])
                low[k, p] = cr * e0 - br * e1
                low[k, p + 1] = ar * e1 - br * e0
                for h in range(k // 8, H):
                    cs[k, h] = cs[k, h] - (cs[p, h] * low[k, p] + cs[p + 1, h] * low[k, p + 1])
            r0, r1 = full(rows[hp][s : s + 1, :]), full(rows[hp][s + 1 : s + 2, :])
            x0, x1 = cr * r0 - br * r1, ar * r1 - br * r0
            begun[p], begun[p + 1] = x0, x1
            fixes.append((hp, s, ratio * r0))
            for h in range(hp, H):
                if h == hp and s == 6:
                    continue
                f0, f1 = cs[p, h], cs[p + 1, h]
                if h == hp:
                    f0, f1 = jnp.where(sub > s + 1, f0, 0.0), jnp.where(sub > s + 1, f1, 0.0)
                rows[h] = rows[h] - (f0 * x0 + f1 * x1)
        back = [None] * W
        for p in reversed(range(W)):
            v = begun[p]
            for i in reversed(range(p // 2 * 2 + 2, W)):
                v = v - low[i, p] * back[i]
            back[p] = v
        far = q + 2 * H
        for i in range(q + H, min(far, B // 8)):
            terms = [column(tiles[i], j + p) * back[p] for p in range(W)]
            tiles[i] = jnp.where(here, 0.0, tiles[i]) - tree(terms)
        if far < B // 8:
            packed = []
            for h in range(H):
                v = back[8 * h]
                for s in range(1, 8):
                    v = jnp.where(sub == s, back[8 * h + s], v)
                packed.append(v)
            zh, zl = split(jnp.concatenate(tiles[far:], axis=0)[:, j : j + W])
            ph, pq = split(jnp.concatenate(packed, axis=0))
            drop = dot3(zh, zl, ph, pq, 1, 0)
            for i in range(far, B // 8):
                k = 8 * (i - far)
                tiles[i] = jnp.where(here, 0.0, tiles[i]) - drop[k : k + 8, :]
        for h, s, fix in fixes:
            rows[h] = jnp.where(sub == s + 1, rows[h] - fix, rows[h])
        for h in range(H):
            scale = pivots[8 * h]
            for s in range(1, 8):
                scale = jnp.where(sub == s, pivots[8 * h + s], scale)
            tiles[q + h] = rows[h] * lax.rsqrt(scale)
    w = jnp.concatenate(tiles, axis=0)
    r = lax.broadcasted_iota(jnp.int32, (B, B), 0)
    c = lax.broadcasted_iota(jnp.int32, (B, B), 1)
    return jnp.where(r >= c, w, 0.0)


SIDE = GC + B


def dot3(ah, al, bh, bl, ca, cb):
    return dot(ah, bh, ca, cb) + (dot(ah, bl, ca, cb) + dot(al, bh, ca, cb))


def block_of(k):
    return pl.ds(pl.multiple_of(k * B, B), B)


DIAG, PICK, CROSS, REST = 0, 1, 2, 3
PARTS = (
    (slice(COLS, LEFT), slice(0, PG)),
    (slice(COLS, LEFT), slice(PG, RIGHT)),
    (slice(0, COLS), slice(0, PG)),
    (slice(0, COLS), slice(PG, RIGHT)),
)


def step_kernel(
    tx_ref, rx_ref, layer_ref, cond_ref, tx_list, rx_list, damp_list, order,
    trail_ref, factor_ref,
    part_ref, diag_part, damp_ref, layers, held, conds, sens, tx_hot, rx_hot, tx_pick, rx_pick,
    gr_send, gr_recv, gc_send, gc_recv, gp_send, gp_recv, local,
    now, acc, nxt, high, low, wh, wl, xh, xl, got, diag, side_rows, cross,
    rs_send, rs_recv, dz_send, dz_recv, dy_send, dy_recv, dx_send, dx_recv, dp_send, dp_recv,
    cz_send, cz_recv, cy_send, cy_recv, ex_send, ex_recv, ep_send, ep_recv,
):
    x, c, z, y = places()
    g = x * NCORE + c
    pair = {"grp": x * NCORE + 1 - c}
    at_y = [None] + [{"tile": z * NY + lax.rem(y + d, NY)} for d in range(1, NY)]
    at_x = [None] + [{"grp": lax.rem(x + d, NX) * NCORE + c} for d in range(1, NX)]
    in_z = [None] + [{"tile": lax.rem(z + d, NZ) * NY + y} for d in range(1, NZ)]
    greet(at_y[1:] + at_x[1:] + in_z[1:] + [pair])

    def prep():
        prepare(
            tx_list, rx_list, damp_list, order, tx_hot, rx_hot, tx_pick, rx_pick, damp_ref,
            g, z, y, z * NY + y,
        )

    everything, finish = gram_part(
        tx_ref, rx_ref, layer_ref, cond_ref, prep, part_ref, diag_part, layers, held, conds, sens,
        tx_hot, rx_hot, tx_pick, rx_pick,
        gr_send, gr_recv, gc_send, gc_recv, gp_send, gp_recv, local,
    )

    def rs(p, d):
        rows, cols = PARTS[p]
        there = lax.rem(y + d, NY)
        return sends(
            diag_part.at[there] if p == DIAG else part_ref.at[there, rows, cols], got.at[d - 1, rows, cols],
            rs_send.at[p, d], rs_recv.at[p, d], at_y[d],
        )

    def start_sums(p):
        for d in range(1, NY):
            rs(p, d).start()

    def summed(p):
        rows, cols = PARTS[p]
        total = diag_part[y] if p == DIAG else part_ref[y, rows, cols]
        for d in range(1, NY):
            rs(p, d).wait_recv()
            total += got[d - 1, rows, cols]
        return total * (1.0 / NCELLS) + damp_ref[rows, cols]

    def dz(d):
        return sends(diag.at[g, z, y], diag.at[g, z, y], dz_send.at[d], dz_recv.at[d], in_z[d])

    def dy(zz, d):
        return sends(diag.at[g, zz, y], diag.at[g, zz, y], dy_send.at[zz, d], dy_recv.at[zz, d], at_y[d])

    def dx(zz, d):
        return sends(diag.at[g, zz], diag.at[g, zz], dx_send.at[zz, d], dx_recv.at[zz, d], at_x[d])

    def dp(zz, d):
        gd = lax.rem(x + NX - d, NX) * NCORE + c
        return sends(diag.at[gd, zz], diag.at[gd, zz], dp_send.at[zz, d], dp_recv.at[zz, d], pair)

    def cz(d):
        return sends(side_rows.at[z, y], side_rows.at[z, y], cz_send.at[d], cz_recv.at[d], in_z[d])

    def cy(zz, d):
        return sends(side_rows.at[zz, y], side_rows.at[zz, y], cy_send.at[zz, d], cy_recv.at[zz, d], at_y[d])

    def ex(d):
        return sends(cross.at[g], cross.at[g], ex_send.at[d], ex_recv.at[d], at_x[d])

    def ep(d):
        gd = lax.rem(x + NX - d, NX) * NCORE + c
        return sends(cross.at[gd], cross.at[gd], ep_send.at[d], ep_recv.at[d], pair)

    def arrived(zz, copy, sem_recv, ref):
        d = lax.rem(z + NZ - zz, NZ)

        @pl.when(d != 0)
        def _():
            sends(ref.at[zz, y], ref.at[zz, y], sem_recv.at[d], sem_recv.at[d], pair).wait_recv()

    def across(zz):
        for d in range(1, NX):
            dx(zz, d).wait_recv()
            dp(zz, d).start()

    def complete(zz):
        for d in range(NX):
            dp(zz, d).wait_recv()

    start_sums(DIAG)
    high[...] = jnp.zeros_like(high)
    low[...] = jnp.zeros_like(low)
    xh[...] = jnp.zeros_like(xh)
    xl[...] = jnp.zeros_like(xl)

    def remaining(i, carry):
        everything(i)

        @pl.when(i == 1)
        def _():
            diag[g, z, y] = summed(DIAG)
            for d in range(1, NZ):
                dz(d).start()

        @pl.when(i == 4)
        def _():
            for zz in range(NZ):
                arrived(zz, None, dz_recv, diag.at[g])
                for d in range(1, NY):
                    dy(zz, d).start()

        @pl.when(i == 5)
        def _():
            for zz in range(NZ):
                for d in range(1, NY):
                    dy(zz, d).wait_recv()
                for d in range(1, NX):
                    dx(zz, d).start()
                dp(zz, 0).start()

        return carry

    lax.fori_loop(0, NZ, remaining, 0)
    start_sums(PICK)
    start_sums(CROSS)
    start_sums(REST)
    across(0)
    complete(0)

    def diag_rows(k, begin):
        return jnp.concatenate([diag[i, k].reshape(B, B) for i in range(begin, NG)], axis=1)

    fh, fl = split(inverse_factor(diag[0, 0].reshape(B, B)))
    wh[0] = fh
    wl[0] = fl
    across(1)
    across(2)
    complete(1)
    acc[...] = diag_rows(0, 0)
    nxt[...] = diag_rows(1, 0)
    fvh, fvl = split(dot3(fh, fl, *split(acc[:, B : 2 * B]), 1, 0))
    now[...] = nxt[:, B : 2 * B] - dot3(fvh, fvl, fvh, fvl, 0, 0)
    side_rows[z, y] = summed(PICK)
    for d in range(1, NZ):
        cz(d).start()
    cross[g] = summed(CROSS)
    for d in range(1, NX):
        ex(d).start()
    ep(0).start()

    def block(k, begin, depth):
        w = inverse_factor(now[...])
        last = k - 1
        cols = slice(begin * B, PICKED)
        ah, al = split(acc[:, cols])
        uh, ul = split(dot3(wh[last], wl[last], ah, al, 1, 0))
        high[block_of(last), cols] = uh
        low[block_of(last), cols] = ul
        at = block_of(k)
        acc[:, cols] = nxt[:, cols] - dot3(high[block_of(last), at], low[block_of(last), at], uh, ul, 0, 0)
        after = jnp.minimum(k + 1, NG - 1)
        there = block_of(after)
        nxt[:, cols] = diag_rows(after, begin) - dot3(
            high[0:depth, there], low[0:depth, there], high[0:depth, cols], low[0:depth, cols], 0, 0
        )
        nh, nl = split(w)
        wh[k] = nh
        wl[k] = nl
        bh, bl = split(acc[:, there])
        vh, vl = split(dot3(nh, nl, bh, bl, 1, 0))
        now[...] = nxt[:, there] - dot3(vh, vl, vh, vl, 0, 0)

    def side(i, depth):
        at = block_of(i)
        padded = jnp.concatenate([cross[i], jnp.zeros((B - COLS, B), F32)], axis=0).T
        start = jnp.concatenate([side_rows[i].reshape(B, GC), padded], axis=1)
        done = dot3(high[0:depth, at], low[0:depth, at], xh[0:depth, :], xl[0:depth, :], 0, 0)
        sh, sl = split(start - done)
        u = dot3(wh[i], wl[i], sh, sl, 1, 0)
        uh, ul = split(u)
        xh[at, :] = uh
        xl[at, :] = ul
        factor_ref[:, at] = u[:, 0:GC].T[0:ROWS, :]

    def first(k, carry):
        across(k + 2)
        complete(k + 1)

        @pl.when(k == 2)
        def _():
            for zz in range(NZ):
                arrived(zz, None, cz_recv, side_rows)
                for d in range(1, NY):
                    cy(zz, d).start()
            for d in range(1, NX):
                ex(d).wait_recv()
                ep(d).start()

        block(k, 0, 4 * B)
        return carry

    def here(i):
        for d in range(1, NY):
            cy(i, d).wait_recv()

    def second(k, carry):
        across(k + 2)
        complete(k + 1)
        i = 2 * (k - 4)
        here(i)
        here(i + 1)
        block(k, 3, 5 * B)
        side(i, 4 * B)
        side(i + 1, 4 * B)
        return carry

    def third(k, carry):
        @pl.when(k < NG - 1)
        def _():
            complete(k + 1)

        here(k - 2)
        block(k, 5, 7 * B)
        side(k - 2, 6 * B)
        return carry

    lax.fori_loop(1, 4, first, 0)
    for d in range(NX):
        ep(d).wait_recv()
    lax.fori_loop(4, 6, second, 0)
    lax.fori_loop(6, NG, third, 0)
    here(NG - 2)
    here(NG - 1)
    side(NG - 2, 6 * B)
    side(NG - 1, 7 * B)
    drop = dot3(xh[:, GC:], xl[:, GC:], xh[:, 0:GC], xl[:, 0:GC], 0, 0)
    trail_ref[...] = (summed(REST) - drop[0:COLS, :])[:, 0:ROWS]

    finish()
    for d in range(1, NY):
        for p in range(4):
            rs(p, d).wait_send()
        for zz in range(NZ):
            dy(zz, d).wait_send()
            cy(zz, d).wait_send()
    for d in range(1, NZ):
        dz(d).wait_send()
        cz(d).wait_send()
    for d in range(NX):
        for zz in range(NZ):
            if d:
                dx(zz, d).wait_send()
            dp(zz, d).wait_send()
        if d:
            ex(d).wait_send()
        ep(d).wait_send()


def shards(
    tx_fields, rx_fields, layer_of_cell, layer_cond, tx_of_row, rx_of_row, damping, panel_order
):
    lists = [
        jnp.pad(v, (0, LINES * 128 - M)).reshape(LINES, 128)
        for v in (tx_of_row, rx_of_row, damping, panel_order)
    ]
    vmem = pl.BlockSpec(memory_space=VMEM)
    smem = pl.BlockSpec(memory_space=pltpu.SMEM)
    hbm = pl.BlockSpec(memory_space=pltpu.HBM)
    trailing, factor = pl.pallas_call(
        step_kernel,
        out_shape=(
            jax.ShapeDtypeStruct((COLS, ROWS), F32),
            jax.ShapeDtypeStruct((ROWS, PICKED), F32),
        ),
        in_specs=[hbm, hbm, hbm, smem, vmem, vmem, vmem, vmem],
        out_specs=(vmem, vmem),
        scratch_shapes=[
            VMEM((NY, LEFT, RIGHT), F32),
            VMEM((NY, PT, PG), F32),
            VMEM((LEFT, RIGHT), F32),
            VMEM((CELLS // 128, 128), jnp.int32),
            VMEM((NZ, NCORE, MSGS, 32, CELLS), BF16),
            VMEM((NZ, 1, CELLS), F32),
            VMEM((RIGHT + NY * LEFT, CELLS), BF16),
            VMEM((RIGHT + NY * LEFT, 128), BF16),
            VMEM((RIGHT + NY * LEFT, 128), BF16),
            VMEM((2 * PG, 128), BF16),
            VMEM((2 * PG, 128), BF16),
        ]
        + [DMA((NZ, MSGS))] * 2
        + [DMA((NZ,))] * 2
        + [DMA((NZ, MSGS))] * 2
        + [DMA((NCORE, MSGS + 1))]
        + [
            VMEM((B, B), F32),
            VMEM((B, PICKED), F32),
            VMEM((B, PICKED), F32),
            VMEM((PICKED, PICKED), BF16),
            VMEM((PICKED, PICKED), BF16),
            VMEM((NG, B, B), BF16),
            VMEM((NG, B, B), BF16),
            VMEM((PICKED, SIDE), BF16),
            VMEM((PICKED, SIDE), BF16),
            VMEM((NY - 1, LEFT, RIGHT), F32),
            VMEM((NG, NZ, NY, PT, PG), F32),
            VMEM((NZ, NY, PT, GC), F32),
            VMEM((NG, COLS, PG), F32),
        ]
        + [DMA((4, NY))] * 2
        + [DMA((NZ,))] * 2
        + [DMA((NZ, NY))] * 2
        + [DMA((NZ, NX))] * 4
        + [DMA((NZ,))] * 2
        + [DMA((NZ, NY))] * 2
        + [DMA((NX,))] * 4,
        compiler_params=pltpu.CompilerParams(
            collective_id=0, has_side_effects=True, vmem_limit_bytes=34 << 20
        ),
        name="step",
    )(
        *(
            pltpu.with_memory_space_constraint(v, pltpu.HBM)
            for v in (tx_fields, rx_fields, layer_of_cell.reshape(-1, 128))
        ),
        layer_cond,
        *lists,
    )
    return trailing.T, factor


def solution(mesh):
    placed = (P(None, "tile"), P(None, "tile"), P("tile"), P(), P(), P(), P(), P())
    return jax.shard_map(
        shards,
        mesh=mesh,
        in_specs=placed,
        out_specs=(P("grp", "tile"), P("grp", None)),
        check_vma=False,
    )
```

```python
import functools

import jax
import jax.numpy as jnp
from jax import lax
from jax.experimental import pallas as pl
from jax.experimental.pallas import tpu as pltpu
from jax.sharding import PartitionSpec as P

F32 = jnp.float32
BF16 = jnp.bfloat16
MESH = pl.DeviceIdType.MESH
VMEM = pltpu.VMEM
DMA = pltpu.SemaphoreType.DMA

M = 2816
NCELLS = 32768
PICKED = 1024
NX, NY, NZ, NCORE = 4, 4, 8, 2
NG = NX * NCORE
NT = NY * NZ
ROWS = M // NG
COLS = M // NT
PG = PICKED // NG
PT = PICKED // NT
CELLS = NCELLS // NT
RIGHT = 512
LEFT = COLS + PT
B = 128
GC = RIGHT - PG


def dot(a, b, ca, cb):
    return lax.dot_general(a, b, (((ca,), (cb,)), ((), ())), preferred_element_type=F32)


def split(x):
    hi = x.astype(BF16)
    return hi, (x - hi.astype(F32)).astype(BF16)


def places():
    g = lax.axis_index("grp")
    t = lax.axis_index("tile")
    return g // NCORE, g % NCORE, t // NY, t % NY


def at_z(z, y):
    return {"tile": lax.rem(z + NZ, NZ) * NY + y}


def greet(peers):
    barrier = pltpu.get_barrier_semaphore()
    for peer in peers:
        pl.semaphore_signal(barrier, inc=1, device_id=peer, device_id_type=MESH)
    pl.semaphore_wait(barrier, len(peers))


def sends(src, dst, send, recv, peer):
    return pltpu.make_async_remote_copy(
        src_ref=src, dst_ref=dst, send_sem=send, recv_sem=recv, device_id=peer, device_id_type=MESH
    )


def owner_of(z, i):
    hops = (i + 1) // 2
    return lax.rem(z + NZ + jnp.where(i % 2 == 1, -hops, hops), NZ)


MSGS = 3
LINES = 24


def look_up(ids, tables):
    count = ids.shape[0]
    lanes = lax.broadcasted_iota(jnp.int32, (count, 128), 1)
    line = jnp.where((ids >> 7) == lanes, 1.0, 0.0).astype(BF16)[:, 0:LINES]
    found = dot(line, jnp.concatenate(tables, axis=1).astype(BF16), 1, 0)
    mine = (ids & 127) == lanes
    return [
        jnp.sum(jnp.where(mine, found[:, 128 * i : 128 * i + 128], 0.0), axis=1, keepdims=True)
        for i in range(len(tables))
    ]


def column(row):
    at = [lax.broadcasted_iota(jnp.int32, (128, 128), d) for d in (0, 1)]
    return jnp.sum(jnp.where(at[0] == at[1], row, 0.0), axis=1, keepdims=True)


def prepare(tx_list, rx_list, damp_list, order, tx_hot, rx_hot, damp, g, z, y, t):
    def run(begin, count):
        return begin + lax.broadcasted_iota(jnp.int32, (count, 1), 0)

    right_row = order[pl.ds(g, 1), :].astype(F32)
    left_picks = column(order[pl.ds(z, 1), :].astype(F32)).astype(jnp.int32)
    ids = [column(right_row).astype(jnp.int32), run(g * ROWS, ROWS), run(0, RIGHT - PG - ROWS) * 0 - 1]
    for j in range(NY):
        ids += [run((z * NY + j) * COLS, COLS), left_picks[PT * j : PT * j + PT, :]]
    ids = jnp.concatenate(ids, axis=0)
    txv, rxv = look_up(ids, [v[...].astype(F32) for v in (tx_list, rx_list)])
    none = jnp.where(ids < 0, -1.0, 0.0)
    lane = lax.broadcasted_iota(jnp.int32, (RIGHT + NY * LEFT, 128), 1).astype(F32)
    tx_hot[...] = jnp.where(txv + none == lane, 1.0, 0.0).astype(BF16)
    rx_hot[...] = jnp.where(rxv + none == lane, 1.0, 0.0).astype(BF16)

    own_picks = sum(jnp.where(y == j, left_picks[PT * j : PT * j + PT, :], 0) for j in range(NY))
    left = jnp.concatenate([run(t * COLS, COLS), own_picks], axis=0)
    table = damp_list[...]
    high = table.astype(BF16).astype(F32)
    mid = (table - high).astype(BF16).astype(F32)
    terms = look_up(left, [high, mid, table - high - mid])
    near = terms[0] + (terms[1] + terms[2])
    natural = lax.broadcasted_iota(jnp.int32, (1, GC), 1)
    natural = jnp.where(natural < ROWS, g * ROWS + natural, -1)
    right = jnp.concatenate([right_row.astype(jnp.int32), natural], axis=1)
    damp[...] = jnp.where(left == right, near, 0.0)


def gram_part(
    tx_ref, rx_ref, layer_ref, cond_ref, prep, part, layers, held, conds, sens, tx_hot, rx_hot,
    ring_send, ring_recv, cond_send, cond_recv, pair_send, pair_recv, local,
):
    x, c, z, y = places()
    up, down, pair = at_z(z + 1, y), at_z(z + NZ - 1, y), {"grp": x * NCORE + 1 - c}

    def own(m):
        if m == 0:
            return tx_ref.at[pl.ds(pl.multiple_of(c * 32, 32), 32), :]
        return rx_ref.at[pl.ds(pl.multiple_of(c * 64 + (m - 1) * 32, 32), 32), :]

    def way(i, m):
        return i % 2 == 1 if i < NZ - 1 else m == 0

    def ring(i, m):
        first = i < 3
        rising = way(i, m)
        prior = i - 2 if i < NZ - 1 or rising else i - 1
        o = z if first else owner_of(z, prior)
        src = own(m) if first else held.at[o, c, m]
        return sends(src, held.at[o, c, m], ring_send.at[i, m], ring_recv.at[i, m], up if rising else down)

    def line(i):
        o = z if i < 3 else owner_of(z, i - 2)
        return sends(conds.at[o], conds.at[o], cond_send.at[i], cond_recv.at[i], up if i % 2 == 1 else down)

    def to_pair(i, m):
        o = owner_of(z, i)
        return sends(held.at[o, c, m], held.at[o, c, m], pair_send.at[i, m], pair_recv.at[i, m], pair)

    def arrive(i, m):
        ring(i, m).wait_recv()
        if i < NZ - 3:
            ring(i + 2, m).start()
        elif i < NZ - 1 and way(NZ - 1, m) == (i % 2 == 1):
            ring(NZ - 1, m).start()
        to_pair(i, m).start()
        if m == 0:
            line(i).wait_recv()
            if i + 2 < NZ:
                line(i + 2).start()

    for m in range(MSGS):
        ring(1, m).start()
        ring(2, m).start()
    mine = []
    for core in range(NCORE):
        mine.append(pltpu.make_async_copy(tx_ref.at[32 * core : 32 * core + 32, :], held.at[z, core, 0], local.at[core, 0]))
        for m in (1, 2):
            at = 64 * core + 32 * (m - 1)
            mine.append(pltpu.make_async_copy(rx_ref.at[at : at + 32, :], held.at[z, core, m], local.at[core, m]))
    mine.append(pltpu.make_async_copy(layer_ref, layers, local.at[0, MSGS]))
    for copy in mine:
        copy.start()
    mine.pop().wait()
    layer = layers[...]
    cond = jnp.zeros(layer.shape, F32)
    for level in range(32):
        cond = jnp.where(layer == level, cond_ref[level], cond)
    conds[z] = jnp.concatenate([cond[r : r + 1, :] for r in range(CELLS // 128)], axis=1)
    line(1).start()
    line(2).start()
    prep()
    part[...] = jnp.zeros_like(part)
    for copy in mine:
        copy.wait()
    for m in range(MSGS):
        arrive(1, m)

    def body(i, carry):
        for n in range(NZ - 1):
            @pl.when(i == n)
            def _():
                for m in range(MSGS):
                    if n + 2 < NZ - 1:
                        arrive(n + 2, m)
                    elif way(NZ - 1, m) == (n % 2 == 1):
                        arrive(NZ - 1, m)

        for n in range(1, NZ):
            @pl.when(i == n)
            def _():
                for m in range(MSGS):
                    to_pair(n, m).wait_recv()

        o = owner_of(z, i)
        txs = jnp.concatenate([held[o, k, 0] for k in range(NCORE)], axis=0)
        rxs = jnp.concatenate([held[o, k, m] for k in range(NCORE) for m in (1, 2)], axis=0)
        both = dot(tx_hot[:, 0:64], txs, 1, 0) * dot(rx_hot[...], rxs, 1, 0)
        sens[...] = (both * conds[o]).astype(BF16)
        part[...] += dot(sens[RIGHT:, :], sens[0:RIGHT, :], 1, 1).reshape(NY, LEFT, RIGHT)
        return carry

    lax.fori_loop(0, NZ, body, 0)

    def finish():
        for i in range(1, NZ):
            for m in range(MSGS):
                ring(i, m).wait_send()
                to_pair(i, m).wait_send()
            line(i).wait_send()

    return finish


def tree(vs):
    while len(vs) > 1:
        vs = [vs[i] + vs[i + 1] if i + 1 < len(vs) else vs[i] for i in range(0, len(vs), 2)]
    return vs[0]


def inverse_factor(m):
    W = 16
    H = W // 8
    lane = lax.broadcasted_iota(jnp.int32, (8, B), 1)
    sub = lax.broadcasted_iota(jnp.int32, (8, B), 0)
    tiles = [m[8 * i : 8 * i + 8, :] for i in range(B // 8)]
    full = lambda v: jnp.broadcast_to(v, (8, B))
    column = lambda t, j: jnp.take_along_axis(t, jnp.full((8, B), j, jnp.int32), axis=1)
    for j in range(0, B, W):
        q = j // 8
        here = (lane >= j) & (lane < j + W)
        cs = {}
        for p in range(W):
            for h in range(p // 8, H):
                cs[p, h] = column(tiles[q + h], j + p)
        rows = [
            jnp.where(lane == j + 8 * h + sub, 1.0, jnp.where(here, 0.0, tiles[q + h])) for h in range(H)
        ]
        pivots, begun, low, fixes = {}, [None] * W, {}, []
        for p in range(0, W, 2):
            hp, s = divmod(p, 8)
            c0, c1 = cs[p, hp], cs[p + 1, hp]
            a, b, c = full(c0[s : s + 1, :]), full(c0[s + 1 : s + 2, :]), full(c1[s + 1 : s + 2, :])
            r = 1.0 / (a * c - b * b)
            ar, br, cr = a * r, b * r, c * r
            ratio = b / a
            pivots[p], pivots[p + 1] = a, c - b * ratio
            for k in range(p + 2, W):
                e0 = full(cs[p, k // 8][k % 8 : k % 8 + 1, :])
                e1 = full(cs[p + 1, k // 8][k % 8 : k % 8 + 1, :])
                low[k, p] = cr * e0 - br * e1
                low[k, p + 1] = ar * e1 - br * e0
                for h in range(k // 8, H):
                    cs[k, h] = cs[k, h] - (cs[p, h] * low[k, p] + cs[p + 1, h] * low[k, p + 1])
            r0, r1 = full(rows[hp][s : s + 1, :]), full(rows[hp][s + 1 : s + 2, :])
            x0, x1 = cr * r0 - br * r1, ar * r1 - br * r0
            begun[p], begun[p + 1] = x0, x1
            fixes.append((hp, s, ratio * r0))
            for h in range(hp, H):
                if h == hp and s == 6:
                    continue
                f0, f1 = cs[p, h], cs[p + 1, h]
                if h == hp:
                    f0, f1 = jnp.where(sub > s + 1, f0, 0.0), jnp.where(sub > s + 1, f1, 0.0)
                rows[h] = rows[h] - (f0 * x0 + f1 * x1)
        back = [None] * W
        for p in reversed(range(W)):
            v = begun[p]
            for i in reversed(range(p // 2 * 2 + 2, W)):
                v = v - low[i, p] * back[i]
            back[p] = v
        far = q + 2 * H
        for i in range(q + H, min(far, B // 8)):
            terms = [column(tiles[i], j + p) * back[p] for p in range(W)]
            tiles[i] = jnp.where(here, 0.0, tiles[i]) - tree(terms)
        if far < B // 8:
            packed = []
            for h in range(H):
                v = back[8 * h]
                for s in range(1, 8):
                    v = jnp.where(sub == s, back[8 * h + s], v)
                packed.append(v)
            zh, zl = split(jnp.concatenate(tiles[far:], axis=0)[:, j : j + W])
            ph, pq = split(jnp.concatenate(packed, axis=0))
            drop = dot3(zh, zl, ph, pq, 1, 0)
            for i in range(far, B // 8):
                k = 8 * (i - far)
                tiles[i] = jnp.where(here, 0.0, tiles[i]) - drop[k : k + 8, :]
        for h, s, fix in fixes:
            rows[h] = jnp.where(sub == s + 1, rows[h] - fix, rows[h])
        for h in range(H):
            scale = pivots[8 * h]
            for s in range(1, 8):
                scale = jnp.where(sub == s, pivots[8 * h + s], scale)
            tiles[q + h] = rows[h] * lax.rsqrt(scale)
    w = jnp.concatenate(tiles, axis=0)
    r = lax.broadcasted_iota(jnp.int32, (B, B), 0)
    c = lax.broadcasted_iota(jnp.int32, (B, B), 1)
    return jnp.where(r >= c, w, 0.0)


SIDE = GC + B


def dot3(ah, al, bh, bl, ca, cb):
    return dot(ah, bh, ca, cb) + (dot(ah, bl, ca, cb) + dot(al, bh, ca, cb))


def block_of(k):
    return pl.ds(pl.multiple_of(k * B, B), B)


DIAG, PICK, CROSS, REST = 0, 1, 2, 3
PARTS = (
    (slice(COLS, LEFT), slice(0, PG)),
    (slice(COLS, LEFT), slice(PG, RIGHT)),
    (slice(0, COLS), slice(0, PG)),
    (slice(0, COLS), slice(PG, RIGHT)),
)


def step_kernel(
    tx_ref, rx_ref, layer_ref, cond_ref, tx_list, rx_list, damp_list, order,
    trail_ref, factor_ref,
    part_ref, damp_ref, layers, held, conds, sens, tx_hot, rx_hot,
    gr_send, gr_recv, gc_send, gc_recv, gp_send, gp_recv, local,
    now, acc, nxt, high, low, wh, wl, xh, xl, got, diag, side_rows, cross,
    rs_send, rs_recv, dz_send, dz_recv, dy_send, dy_recv, dx_send, dx_recv, dp_send, dp_recv,
    cz_send, cz_recv, cy_send, cy_recv, ex_send, ex_recv, ep_send, ep_recv,
):
    x, c, z, y = places()
    g = x * NCORE + c
    pair = {"grp": x * NCORE + 1 - c}
    at_y = [None] + [{"tile": z * NY + lax.rem(y + d, NY)} for d in range(1, NY)]
    at_x = [None] + [{"grp": lax.rem(x + d, NX) * NCORE + c} for d in range(1, NX)]
    in_z = [None] + [{"tile": lax.rem(z + d, NZ) * NY + y} for d in range(1, NZ)]
    greet(at_y[1:] + at_x[1:] + in_z[1:] + [pair])

    def prep():
        prepare(tx_list, rx_list, damp_list, order, tx_hot, rx_hot, damp_ref, g, z, y, z * NY + y)

    finish = gram_part(
        tx_ref, rx_ref, layer_ref, cond_ref, prep, part_ref, layers, held, conds, sens, tx_hot, rx_hot,
        gr_send, gr_recv, gc_send, gc_recv, gp_send, gp_recv, local,
    )

    def rs(p, d):
        rows, cols = PARTS[p]
        return sends(
            part_ref.at[lax.rem(y + d, NY), rows, cols], got.at[d - 1, rows, cols],
            rs_send.at[p, d], rs_recv.at[p, d], at_y[d],
        )

    def start_sums(p):
        for d in range(1, NY):
            rs(p, d).start()

    def summed(p):
        rows, cols = PARTS[p]
        total = part_ref[y, rows, cols]
        for d in range(1, NY):
            rs(p, d).wait_recv()
            total += got[d - 1, rows, cols]
        return total * (1.0 / NCELLS) + damp_ref[rows, cols]

    def dz(d):
        return sends(diag.at[g, z, y], diag.at[g, z, y], dz_send.at[d], dz_recv.at[d], in_z[d])

    def dy(zz, d):
        return sends(diag.at[g, zz, y], diag.at[g, zz, y], dy_send.at[zz, d], dy_recv.at[zz, d], at_y[d])

    def dx(zz, d):
        return sends(diag.at[g, zz], diag.at[g, zz], dx_send.at[zz, d], dx_recv.at[zz, d], at_x[d])

    def dp(zz, d):
        gd = lax.rem(x + NX - d, NX) * NCORE + c
        return sends(diag.at[gd, zz], diag.at[gd, zz], dp_send.at[zz, d], dp_recv.at[zz, d], pair)

    def cz(d):
        return sends(side_rows.at[z, y], side_rows.at[z, y], cz_send.at[d], cz_recv.at[d], in_z[d])

    def cy(zz, d):
        return sends(side_rows.at[zz, y], side_rows.at[zz, y], cy_send.at[zz, d], cy_recv.at[zz, d], at_y[d])

    def ex(d):
        return sends(cross.at[g], cross.at[g], ex_send.at[d], ex_recv.at[d], at_x[d])

    def ep(d):
        gd = lax.rem(x + NX - d, NX) * NCORE + c
        return sends(cross.at[gd], cross.at[gd], ep_send.at[d], ep_recv.at[d], pair)

    def arrived(zz, copy, sem_recv, ref):
        d = lax.rem(z + NZ - zz, NZ)

        @pl.when(d != 0)
        def _():
            sends(ref.at[zz, y], ref.at[zz, y], sem_recv.at[d], sem_recv.at[d], pair).wait_recv()

    def across(zz):
        for d in range(1, NX):
            dx(zz, d).wait_recv()
            dp(zz, d).start()

    def complete(zz):
        for d in range(NX):
            dp(zz, d).wait_recv()

    start_sums(DIAG)
    high[...] = jnp.zeros_like(high)
    low[...] = jnp.zeros_like(low)
    xh[...] = jnp.zeros_like(xh)
    xl[...] = jnp.zeros_like(xl)
    diag[g, z, y] = summed(DIAG)
    for d in range(1, NZ):
        dz(d).start()
    for zz in range(NZ):
        arrived(zz, None, dz_recv, diag.at[g])
        for d in range(1, NY):
            dy(zz, d).start()
    for zz in range(NZ):
        for d in range(1, NY):
            dy(zz, d).wait_recv()
        for d in range(1, NX):
            dx(zz, d).start()
        dp(zz, 0).start()
    start_sums(PICK)
    start_sums(CROSS)
    start_sums(REST)
    across(0)
    complete(0)

    def diag_rows(k, begin):
        return jnp.concatenate([diag[i, k].reshape(B, B) for i in range(begin, NG)], axis=1)

    fh, fl = split(inverse_factor(diag[0, 0].reshape(B, B)))
    wh[0] = fh
    wl[0] = fl
    across(1)
    across(2)
    complete(1)
    acc[...] = diag_rows(0, 0)
    nxt[...] = diag_rows(1, 0)
    fvh, fvl = split(dot3(fh, fl, *split(acc[:, B : 2 * B]), 1, 0))
    now[...] = nxt[:, B : 2 * B] - dot3(fvh, fvl, fvh, fvl, 0, 0)
    side_rows[z, y] = summed(PICK)
    for d in range(1, NZ):
        cz(d).start()
    cross[g] = summed(CROSS)
    for d in range(1, NX):
        ex(d).start()
    ep(0).start()

    def block(k, begin, depth):
        w = inverse_factor(now[...])
        last = k - 1
        cols = slice(begin * B, PICKED)
        ah, al = split(acc[:, cols])
        uh, ul = split(dot3(wh[last], wl[last], ah, al, 1, 0))
        high[block_of(last), cols] = uh
        low[block_of(last), cols] = ul
        at = block_of(k)
        acc[:, cols] = nxt[:, cols] - dot3(high[block_of(last), at], low[block_of(last), at], uh, ul, 0, 0)
        after = jnp.minimum(k + 1, NG - 1)
        there = block_of(after)
        nxt[:, cols] = diag_rows(after, begin) - dot3(
            high[0:depth, there], low[0:depth, there], high[0:depth, cols], low[0:depth, cols], 0, 0
        )
        nh, nl = split(w)
        wh[k] = nh
        wl[k] = nl
        bh, bl = split(acc[:, there])
        vh, vl = split(dot3(nh, nl, bh, bl, 1, 0))
        now[...] = nxt[:, there] - dot3(vh, vl, vh, vl, 0, 0)

    def side(i, depth):
        at = block_of(i)
        padded = jnp.concatenate([cross[i], jnp.zeros((B - COLS, B), F32)], axis=0).T
        start = jnp.concatenate([side_rows[i].reshape(B, GC), padded], axis=1)
        done = dot3(high[0:depth, at], low[0:depth, at], xh[0:depth, :], xl[0:depth, :], 0, 0)
        sh, sl = split(start - done)
        u = dot3(wh[i], wl[i], sh, sl, 1, 0)
        uh, ul = split(u)
        xh[at, :] = uh
        xl[at, :] = ul
        factor_ref[:, at] = u[:, 0:GC].T[0:ROWS, :]

    def first(k, carry):
        across(k + 2)
        complete(k + 1)

        @pl.when(k == 2)
        def _():
            for zz in range(NZ):
                arrived(zz, None, cz_recv, side_rows)
                for d in range(1, NY):
                    cy(zz, d).start()
            for d in range(1, NX):
                ex(d).wait_recv()
                ep(d).start()

        block(k, 0, 4 * B)
        return carry

    def here(i):
        for d in range(1, NY):
            cy(i, d).wait_recv()

    def second(k, carry):
        across(k + 2)
        complete(k + 1)
        i = 2 * (k - 4)
        here(i)
        here(i + 1)
        block(k, 3, 5 * B)
        side(i, 4 * B)
        side(i + 1, 4 * B)
        return carry

    def third(k, carry):
        @pl.when(k < NG - 1)
        def _():
            complete(k + 1)

        here(k - 2)
        block(k, 5, 7 * B)
        side(k - 2, 6 * B)
        return carry

    lax.fori_loop(1, 4, first, 0)
    for d in range(NX):
        ep(d).wait_recv()
    lax.fori_loop(4, 6, second, 0)
    lax.fori_loop(6, NG, third, 0)
    here(NG - 2)
    here(NG - 1)
    side(NG - 2, 6 * B)
    side(NG - 1, 7 * B)
    drop = dot3(xh[:, GC:], xl[:, GC:], xh[:, 0:GC], xl[:, 0:GC], 0, 0)
    trail_ref[...] = (summed(REST) - drop[0:COLS, :])[:, 0:ROWS]

    finish()
    for d in range(1, NY):
        for p in range(4):
            rs(p, d).wait_send()
        for zz in range(NZ):
            dy(zz, d).wait_send()
            cy(zz, d).wait_send()
    for d in range(1, NZ):
        dz(d).wait_send()
        cz(d).wait_send()
    for d in range(NX):
        for zz in range(NZ):
            if d:
                dx(zz, d).wait_send()
            dp(zz, d).wait_send()
        if d:
            ex(d).wait_send()
        ep(d).wait_send()


def shards(
    tx_fields, rx_fields, layer_of_cell, layer_cond, tx_of_row, rx_of_row, damping, panel_order
):
    lists = [
        jnp.pad(v, (0, LINES * 128 - M)).reshape(LINES, 128)
        for v in (tx_of_row, rx_of_row, damping, panel_order)
    ]
    vmem = pl.BlockSpec(memory_space=VMEM)
    smem = pl.BlockSpec(memory_space=pltpu.SMEM)
    hbm = pl.BlockSpec(memory_space=pltpu.HBM)
    trailing, factor = pl.pallas_call(
        step_kernel,
        out_shape=(
            jax.ShapeDtypeStruct((COLS, ROWS), F32),
            jax.ShapeDtypeStruct((ROWS, PICKED), F32),
        ),
        in_specs=[hbm, hbm, hbm, smem, vmem, vmem, vmem, vmem],
        out_specs=(vmem, vmem),
        scratch_shapes=[
            VMEM((NY, LEFT, RIGHT), F32),
            VMEM((LEFT, RIGHT), F32),
            VMEM((CELLS // 128, 128), jnp.int32),
            VMEM((NZ, NCORE, MSGS, 32, CELLS), BF16),
            VMEM((NZ, 1, CELLS), F32),
            VMEM((RIGHT + NY * LEFT, CELLS), BF16),
            VMEM((RIGHT + NY * LEFT, 128), BF16),
            VMEM((RIGHT + NY * LEFT, 128), BF16),
        ]
        + [DMA((NZ, MSGS))] * 2
        + [DMA((NZ,))] * 2
        + [DMA((NZ, MSGS))] * 2
        + [DMA((NCORE, MSGS + 1))]
        + [
            VMEM((B, B), F32),
            VMEM((B, PICKED), F32),
            VMEM((B, PICKED), F32),
            VMEM((PICKED, PICKED), BF16),
            VMEM((PICKED, PICKED), BF16),
            VMEM((NG, B, B), BF16),
            VMEM((NG, B, B), BF16),
            VMEM((PICKED, SIDE), BF16),
            VMEM((PICKED, SIDE), BF16),
            VMEM((NY - 1, LEFT, RIGHT), F32),
            VMEM((NG, NZ, NY, PT, PG), F32),
            VMEM((NZ, NY, PT, GC), F32),
            VMEM((NG, COLS, PG), F32),
        ]
        + [DMA((4, NY))] * 2
        + [DMA((NZ,))] * 2
        + [DMA((NZ, NY))] * 2
        + [DMA((NZ, NX))] * 4
        + [DMA((NZ,))] * 2
        + [DMA((NZ, NY))] * 2
        + [DMA((NX,))] * 4,
        compiler_params=pltpu.CompilerParams(
            collective_id=0, has_side_effects=True, vmem_limit_bytes=34 << 20
        ),
        name="step",
    )(
        *(
            pltpu.with_memory_space_constraint(v, pltpu.HBM)
            for v in (tx_fields, rx_fields, layer_of_cell.reshape(-1, 128))
        ),
        layer_cond,
        *lists,
    )
    return trailing.T, factor


def solution(mesh):
    placed = (P(None, "tile"), P(None, "tile"), P("tile"), P(), P(), P(), P(), P())
    return jax.shard_map(
        shards,
        mesh=mesh,
        in_specs=placed,
        out_specs=(P("grp", "tile"), P("grp", None)),
        check_vma=False,
    )
```
